128 devices in a mesh: gx: 4 (over y), gy: 32 (over x, z, core).
Axes of the slice: x: 4, y: 4, z: 4, core: 2. Of those that a mesh axis runs over, the one named last changes fastest.
Arguments:
- fluid_state: float32 [4, 32, 256, 512], P(None, None, 'gy', 'gx'), may hold values from -6 to 6
- particle_pos: float32 [3, 1048576], P(None, ('gx', 'gy')), may hold values from -6 to 6
- particle_motion: float32 [6, 1048576], P(None, ('gx', 'gy')), may hold values from -6 to 6
- particle_radius: float32 [1048576], P(('gx', 'gy')), may hold values from 0.5 to 1
- particle_temp: float32 [1048576], P(('gx', 'gy')), may hold values from -6 to 6
- particle_cell: int32 [1048576], P(('gx', 'gy')), may hold values from 0 to 32767
- particle_box: int32 [1048576, 1], P(('gx', 'gy')), may hold values from 0 to 127; in each aligned block of 8192 rows (0 to 8191, 8192 to 16383, ...) at most 128 rows name the same one
- box_owner: int32 [128], replicated, may hold values from 0 to 127, each once
- contact_mask: int32 [16384, 128, 128], P(('gx', 'gy')), may hold values 0 or 1
Outputs:
- fluid_next: float32 [4, 32, 256, 512], P(None, None, 'gy', 'gx')
- void_fraction: float32 [32, 256, 512], P(None, 'gy', 'gx')
- particle_next: float32 [7, 1048576], P(None, ('gx', 'gy'))
The draws below stay inside these ranges and needn't reach their ends.
Inputs may be any that keep to these rules, and one draw needn't show every extreme that they name: `particle_box`: among the 8192 rows of one device no box is named by more than 128 rows, a bound that some block reaches. `box_owner`: A permutation of the devices.
All inputs are finite; a program needn't handle non-finite values. No bound on the sum of `contact_mask` on one device may be relied on, other than what follows from the above.
Results may differ from the reference program's by a relative error of at most 0.0003.
Values sent between devices are 32-bit elements; how exact they have to be, the bound alone decides.
A program may use at most 64 MiB of HBM per device.

```python
import math
import jax
import jax.numpy as jnp
import numpy as np
from jax import lax

CX = 128
CY = 8
NZ = 32
P_DEV = 8192
BLOCK = 128
C = 128
NX = 512
NY = 256
NPART = 1048576
NBLK = 16384
CELLS_DEV = 32768
N_GX = 4
N_GY = 32
DEVICES = 128


def touch_ends(values, key, smallest, high):
    extent = values.shape
    spot = [jax.random.randint(jax.random.fold_in(key, axis), (), 0, extent[axis]) for axis in range(len(extent))]
    values = values.at[tuple(spot)].set(smallest)
    longest = extent.index(max(extent))
    spot[longest] = (spot[longest] + 1) % extent[longest]
    return values.at[tuple(spot)].set(high)


def steps_of(rng, shape, cuts, low, largest):
    def one(dim, blocks):
        steps = jax.random.uniform(jax.random.fold_in(jax.random.fold_in(rng, 6), dim), (blocks,), jnp.float32, low / len(cuts), largest / len(cuts))
        return jnp.repeat(jnp.exp(steps), shape[dim] // blocks).reshape((-1,) + (1,) * (len(shape) - dim - 1))

    gain = one(*cuts[0])
    for cut in cuts[1:]:
        gain = gain * one(*cut)
    return gain


def assign_block(rng, own, number, rows, number_of, top, most, skew):
    sequence = jax.random.permutation(rng, number_of)
    packed, usual = load_shares(number_of, rows * top, most, skew, True), load_shares(number_of, rows * top, most, skew, False)
    places = jnp.arange(number_of)

    def named(sizes, offset_by):
        used = int((sizes > 0).sum())
        fixed = max(1, used // 4)
        passed = fixed + (places - fixed + offset_by * (used - fixed)) % max(1, number_of - fixed)
        return jnp.zeros((number_of,), jnp.int32).at[sequence[jnp.where(places < fixed, places, passed)]].set(jnp.asarray(sizes, jnp.int32))

    sizes = jnp.where(number % 4 == 0, named(packed, number // 4), named(usual, number - number // 4 - 1))
    mixed = jax.random.permutation(jax.random.fold_in(own, 3), number_of)
    donor, taker = mixed[0:number_of // 2 * 2:2], mixed[1:number_of // 2 * 2:2]
    slack = jnp.minimum(sizes[donor] - 1, most - sizes[taker]) // 2
    slack = jnp.where((donor == sequence[0]) | (taker == sequence[0]) | (sizes[taker] == 0), 0, jnp.maximum(slack, 0))
    passed = jax.random.randint(jax.random.fold_in(own, 4), (number_of // 2,), 0, 1 << 20) % (slack + 1)
    sizes = sizes.at[donor].add(-passed).at[taker].add(passed)
    labels = jnp.searchsorted(jnp.cumsum(sizes), jnp.arange(rows * top), side="right").astype(jnp.int32)
    grid = labels.reshape(top, rows).T
    grid = grid[jax.random.permutation(jax.random.fold_in(own, 1), rows)]
    offset_by = jax.random.randint(jax.random.fold_in(own, 2), (rows, 1), 0, top)
    return jnp.take_along_axis(grid, (jnp.arange(top)[None, :] + offset_by) % top, axis=1)


def load_shares(number_of, total, bound, lean, full):
    loads = [(1 << 20) // math.isqrt(standing ** lean) + 1 for standing in range(1, number_of + 1)]
    largest = bound if full else min(bound, max(-(-total // number_of), total * loads[0] // sum(loads)))
    least = 1 if total - largest >= number_of - 1 else 0
    counts, rest = [largest] + [least] * (number_of - 1), total - largest - least * (number_of - 1)
    while rest > 0:
        free = [i for i in range(1, number_of) if counts[i] < largest] or [i for i in range(1, number_of) if counts[i] < bound]
        whole, remaining = sum([loads[i] for i in free]), rest
        for i in free:
            more = min(bound - counts[i], max(1, remaining * loads[i] // whole), rest)
            counts[i] = counts[i] + more
            rest = rest - more
    return np.array(counts)


def centred(key, extent, scale, most, cuts=(), kind=jnp.bfloat16):
    factor_of = steps_of(key, extent, cuts, -0.22, 0.18) if cuts else 1.0
    values = jax.random.normal(key, extent, jnp.float32) * scale * factor_of
    return jnp.minimum(jnp.maximum(values, -most), most).astype(kind)


def setup_inputs(seed: int = 0) -> dict:
    key_of = jax.random.split(jax.random.key(seed), 10)
    fluid_state = centred(key_of[0], (4, NZ, NY, NX), 1.0, 6.0, ((2, 32), (3, 4)), jnp.float32)
    particle_pos = centred(key_of[1], (3, NPART), 1.0, 6.0, ((1, 128),), jnp.float32)
    particle_motion = centred(key_of[2], (6, NPART), 1.0, 6.0, ((1, 128),), jnp.float32)
    particle_radius = jnp.clip(0.5 + 0.5 * jax.random.uniform(key_of[3], (NPART,), jnp.float32) ** steps_of(key_of[3], (NPART,), ((0, 128),), -0.2, 0.2), 0.5, 1.0)
    particle_temp = centred(key_of[4], (NPART,), 1.0, 6.0, ((0, 128),), jnp.float32)
    particle_cell = touch_ends(jax.random.randint(key_of[5], (NPART,), 0, CELLS_DEV), jax.random.fold_in(key_of[5], 1), 0, CELLS_DEV - 1).astype(jnp.int32)
    particle_box_keys = jax.random.split(jax.random.fold_in(key_of[6], 1), NPART // P_DEV)
    particle_box_turns = jax.random.permutation(jax.random.fold_in(key_of[6], 3), NPART // P_DEV)
    particle_box = jax.vmap(lambda own, number: assign_block(jax.random.fold_in(key_of[6], 2), own, number, P_DEV, DEVICES, 1, C, 1))(particle_box_keys, particle_box_turns).reshape((NPART, 1))
    box_owner = jax.random.permutation(key_of[7], DEVICES).astype(jnp.int32)
    contact_mask = touch_ends((jax.random.randint(key_of[8], (NBLK, BLOCK, BLOCK), 0, 8) < 1).astype(jnp.int32), jax.random.fold_in(key_of[8], 1), 0, 1)
    return dict(fluid_state=fluid_state, particle_pos=particle_pos, particle_motion=particle_motion, particle_radius=particle_radius, particle_temp=particle_temp, particle_cell=particle_cell, particle_box=particle_box, box_owner=box_owner, contact_mask=contact_mask)


TIME_STEP = 0.1
STIFFNESS = 0.5
DAMPING_RATE = 0.2
ROTATION_DRAG = 0.1
DRAG_COEFF = 4.0
CONDUCTION = 0.3
HEAT_TRANSFER = 4.0
GRAVITY = 0.3
COUPLING = 4.0
CENTRE_WEIGHT = 0.25
SIDE_WEIGHT = 0.125


def smooth(field):
    padded = jnp.pad(field, ((0, 0), (1, 1), (1, 1), (1, 1)))
    interior = padded[:, 1:-1, 1:-1, 1:-1]
    beside_all = padded[:, 2:, 1:-1, 1:-1] + padded[:, :-2, 1:-1, 1:-1]
    beside_all = beside_all + padded[:, 1:-1, 2:, 1:-1] + padded[:, 1:-1, :-2, 1:-1]
    beside_all = beside_all + padded[:, 1:-1, 1:-1, 2:] + padded[:, 1:-1, 1:-1, :-2]
    return CENTRE_WEIGHT * interior + SIDE_WEIGHT * beside_all


def contact(arrived, mask_blocks):
    position = arrived[0:3]
    velocity = arrived[3:6]
    angular = arrived[6:9]
    fluid_vel = arrived[9:12]
    radius = arrived[12]
    solid_temp = arrived[13]
    gas_temp = arrived[14]
    occupied = (radius > 0.0).astype(jnp.float32)
    pair_mask = mask_blocks.astype(jnp.float32) * occupied[:, :, None] * occupied[:, None, :]
    distance = jnp.zeros(pair_mask.shape, jnp.float32)
    for component in range(3):
        offset = position[component][:, :, None] - position[component][:, None, :]
        distance = distance + offset * offset
    reach_sq = (radius[:, :, None] + radius[:, None, :]) ** 2 + 1.0
    weight = pair_mask * jnp.exp(-distance / reach_sq)
    weight_sum = jnp.sum(weight, axis=2)
    stacked = jnp.concatenate([position, velocity, angular, solid_temp[None]], axis=0)
    mixed = jnp.einsum("bij,cbj->cbi", weight, stacked, precision=lax.Precision.HIGHEST)
    spring = position * weight_sum - mixed[0:3]
    damping = velocity * weight_sum - mixed[3:6]
    drag_force = DRAG_COEFF / (radius * radius + 0.25) * (fluid_vel - velocity)
    upward = jnp.array([0.0, 0.0, 1.0], jnp.float32)[:, None, None]
    velocity_next = velocity + TIME_STEP * (STIFFNESS * spring - DAMPING_RATE * damping + drag_force) - TIME_STEP * GRAVITY * upward
    angular_next = angular - TIME_STEP * ROTATION_DRAG * (angular * weight_sum + mixed[6:9])
    temp_next = solid_temp + TIME_STEP * (CONDUCTION * (mixed[9] - solid_temp * weight_sum) + HEAT_TRANSFER * (gas_temp - solid_temp))
    return jnp.concatenate([velocity_next, angular_next, drag_force, temp_next[None]], axis=0)


def reference(fluid_state, particle_pos, particle_motion, particle_radius, particle_temp, particle_cell, particle_box, box_owner, contact_mask):
    devices = N_GX * N_GY
    peer_slots = 2 * P_DEV // devices
    particle_ids = jnp.arange(NPART, dtype=jnp.int32)
    home_dev = particle_ids // P_DEV
    owner_dev = box_owner[particle_box[:, 0]].astype(jnp.int32)
    group_key = (home_dev * devices + owner_dev).astype(jnp.int32)
    sort_order = jnp.argsort(group_key, stable=True).astype(jnp.int32)
    group_counts = jnp.zeros((devices * devices,), jnp.int32).at[group_key].add(1)
    group_starts = jnp.cumsum(group_counts).astype(jnp.int32) - group_counts
    rank_sorted = particle_ids - group_starts[group_key[sort_order]]
    slot_rank = jnp.zeros((NPART,), jnp.int32).at[sort_order].set(rank_sorted)
    target = owner_dev * (2 * P_DEV) + home_dev * peer_slots + slot_rank
    cell_z = particle_cell // (CY * CX)
    cell_y = (particle_cell // CX) % CY
    cell_x = particle_cell % CX
    global_y = (home_dev % N_GY) * CY + cell_y
    global_x = (home_dev // N_GY) * CX + cell_x
    filtered = smooth(fluid_state)
    at_particle = filtered[:, cell_z, global_y, global_x]
    payload = jnp.concatenate([particle_pos, particle_motion, at_particle[0:3], particle_radius[None], particle_temp[None], at_particle[3:4]], axis=0)
    buffer = jnp.zeros((15, 2 * NPART), jnp.float32).at[:, target].set(payload)
    per_block = 2 * P_DEV // BLOCK
    blocks = buffer.reshape(15, devices, per_block, BLOCK).transpose(1, 0, 2, 3)
    mask_blocks = contact_mask.reshape(devices, per_block, BLOCK, BLOCK)

    def contact_pair(pieces):
        return contact(pieces[0], pieces[1])

    result = lax.map(contact_pair, (blocks, mask_blocks))
    result = result.transpose(1, 0, 2, 3).reshape(10, 2 * NPART)
    returned = result[:, target]
    particle_next = jnp.concatenate([returned[0:6], returned[9:10]], axis=0)
    volume = particle_radius ** 3
    deposit_terms = jnp.concatenate([volume[None], -volume[None] * returned[6:9], (volume * (returned[9] - at_particle[3]))[None]], axis=0)
    deposits = jnp.zeros((5, NZ, NY, NX), jnp.float32).at[:, cell_z, global_y, global_x].add(deposit_terms)
    spread = smooth(deposits)
    crowding = 1.0 + COUPLING * spread[0]
    void_fraction = 1.0 / crowding
    fluid_next = jnp.concatenate([fluid_state[0:3] + TIME_STEP * COUPLING * spread[1:4] * crowding, fluid_state[3:4] + TIME_STEP * COUPLING * spread[4:5] * crowding], axis=0)
    return fluid_next, void_fraction, particle_next
```

```python
import functools

import jax
import jax.numpy as jnp
from jax import lax
from jax.experimental import pallas as pl
from jax.experimental.pallas import tpu as pltpu
from jax.sharding import PartitionSpec as P

GX_GY = ("gx", "gy")
LOGICAL = pl.DeviceIdType.LOGICAL
F32, BF16, I32 = jnp.float32, jnp.bfloat16, jnp.int32
DEV = 128
PARTS = 8192
PB = 256
NBLK = PARTS // PB
LOG2E = 1.4426950408889634
VMEM = pltpu.VMEM


def iota(shape, dim):
    return lax.broadcasted_iota(I32, shape, dim)


def hot(mask):
    return jnp.where(mask, 1.0, 0.0).astype(BF16)


def split2(x):
    hi = x.astype(BF16)
    lo = (x - hi.astype(F32)).astype(BF16)
    return hi, lo


def dot_nt(a, b):
    return lax.dot_general(a, b, (((1,), (1,)), ((), ())), preferred_element_type=F32)


def dot_nn(a, b):
    return lax.dot_general(a, b, (((1,), (0,)), ((), ())), preferred_element_type=F32)


def dot_tn(a, b):
    return lax.dot_general(a, b, (((0,), (0,)), ((), ())), preferred_element_type=F32)


def row2(ref, k):
    return jnp.concatenate([ref[pl.ds(2 * k, 1), :], ref[pl.ds(2 * k + 1, 1), :]], axis=1)


def add2(ref, x):
    ref[0] += x[:, :128]
    ref[1] += x[:, 128:]


def place_kernel(
    owner_ref, box_ref, pos_ref, mot_ref, rad_ref, tmp_ref,
    out_ref, q_ref, sc_ref,
    rank_ref, acc_ref, sorted_ref, cnt_ref, smem_ref, sem,
):
    tri = hot(iota((PB, PB), 0) < iota((PB, PB), 1))

    def rank_step(k, before):
        box = row2(box_ref, k)
        match = iota((DEV, PB), 0) == box
        h = hot(match)
        within = dot_nn(h, tri)
        rank = jnp.sum(jnp.where(match, within + before, 0.0), axis=0, keepdims=True)
        rank_ref[pl.ds(2 * k, 1), :] = rank[:, :128]
        rank_ref[pl.ds(2 * k + 1, 1), :] = rank[:, 128:]
        return before + jnp.sum(jnp.where(match, 1.0, 0.0), axis=1, keepdims=True)

    counts = lax.fori_loop(0, NBLK, rank_step, jnp.zeros((DEV, 1), F32))
    wide = jnp.broadcast_to(counts, (DEV, DEV))
    lower = iota((DEV, DEV), 0) < iota((DEV, DEV), 1)
    start_row = jnp.sum(jnp.where(lower, wide, 0.0), axis=0, keepdims=True)
    diag = iota((DEV, DEV), 0) == iota((DEV, DEV), 1)
    count_row = jnp.sum(jnp.where(diag, wide, 0.0), axis=0, keepdims=True)
    sc = jnp.where(iota((8, DEV), 0) == 0, start_row, count_row).astype(I32)
    cnt_ref[...] = sc
    copy = pltpu.make_async_copy(cnt_ref, smem_ref, sem)
    copy.start()
    sc_ref[...] = sc
    table = jnp.broadcast_to(start_row, (64, DEV))
    q = rank_ref[...] + jnp.take_along_axis(table, box_ref[...], axis=1)
    q_ref[...] = q.astype(I32)

    acc_ref[...] = jnp.zeros_like(acc_ref)

    def sort_step(k, carry):
        q = row2(q_ref, k)
        lo_hot = hot(iota((PB, PB), 0) == (q & 255))
        hi_hot = hot(iota((32, PB), 0) == (q >> 8))
        lanes = pl.ds(pl.multiple_of(k * PB, PB), PB)
        rows = [pos_ref[c : c + 1, lanes] for c in range(3)]
        rows += [row2(tmp_ref, k)]
        rows += [mot_ref[c : c + 1, lanes] for c in range(3)]
        rows += [row2(rad_ref, k)]
        rows += [mot_ref[c : c + 1, lanes] for c in range(3, 6)]
        his, los = [], []
        for x in rows:
            hi, lo = split2(jnp.broadcast_to(x, (32, PB)))
            his.append(hi * hi_hot)
            los.append(lo * hi_hot)
        left = jnp.concatenate(
            [jnp.concatenate(his, axis=0), jnp.concatenate(los, axis=0)], axis=1
        )
        right = jnp.concatenate([lo_hot, lo_hot], axis=1)
        add2(acc_ref, dot_nt(left, right))
        return carry

    lax.fori_loop(0, NBLK, sort_step, 0)
    for t in range(64):
        sorted_ref[t, 0:11, :] = acc_ref[t % 2, pl.ds(t // 2, 11, stride=32), :]
    copy.wait()
    lane = iota((16, 128), 1)

    def window(b, carry):
        start = smem_ref[0, b]
        count = smem_ref[1, b]
        tile, off = start >> 7, start & 127
        shift = (128 - off) & 127
        low = pltpu.roll(sorted_ref[tile], shift, 1)
        high = pltpu.roll(sorted_ref[tile + 1], shift, 1)
        both = jnp.where(lane < 128 - off, low, high)
        out_ref[owner_ref[b]] = jnp.where(lane < count, both, 0.0)
        return carry

    lax.fori_loop(0, DEV, window, 0, unroll=4)


def place(box_owner, box, pos, mot, rad, tmp):
    return pl.pallas_call(
        place_kernel,
        out_shape=(
            jax.ShapeDtypeStruct((DEV, 16, 128), F32),
            jax.ShapeDtypeStruct((64, 128), I32),
            jax.ShapeDtypeStruct((8, 128), I32),
        ),
        in_specs=[pl.BlockSpec(memory_space=pltpu.SMEM)] + [pl.BlockSpec(memory_space=VMEM)] * 5,
        out_specs=(pl.BlockSpec(memory_space=VMEM),) * 3,
        scratch_shapes=[
            VMEM((64, 128), F32),
            VMEM((2, 352, 128), F32),
            VMEM((66, 16, 128), F32),
            VMEM((8, 128), I32),
            pltpu.SMEM((8, 128), I32),
            pltpu.SemaphoreType.DMA,
        ],
        name="place",
    )(box_owner, box, pos, mot, rad, tmp)


def contact_block(s, mask):
    sub = iota((8, 128), 0)
    top = s[0:8]
    r = s[7:8]
    occupied = jnp.where(r > 0.0, 1.0, 0.0)
    scale = jnp.where((sub & 3) == 3, 1.4142135623730951, (2.0 * LOG2E) ** 0.5)
    pos4 = jnp.concatenate([s[0:3], r, s[0:3], r], axis=0)
    y = pos4 * scale
    a = y.astype(BF16).astype(F32)
    b = (y - a).astype(BF16).astype(F32)
    c = y - a - b
    first = sub < 4
    is_r = (sub & 3) == 3
    sq = y * y * 0.5
    m = jnp.sum(jnp.where(first & ~is_r, sq, 0.0), axis=0, keepdims=True)
    g = sq[3:4] + 0.5

    def three(v):
        v1 = v.astype(BF16).astype(F32)
        v2 = (v - v1).astype(BF16).astype(F32)
        return v1, v2, v - v1 - v2

    m1, m2, m3 = three(m)
    g1, g2, g3 = three(g)

    def pick(rows):
        out = jnp.zeros((8, 128), F32)
        for i, v in enumerate(rows):
            out = jnp.where(sub == i, v, out)
        return out

    zero = jnp.zeros((8, 128), F32)
    left = jnp.concatenate(
        [a, b, jnp.where(first, a, c), pick([m1, m2, m3, 1.0, 1.0, 1.0]), pick([g1, g2, g3, 1.0, 1.0, 1.0]), zero], axis=0
    ).astype(BF16)
    h1 = jnp.where(first, a, b)
    h3 = jnp.where(first, c, a)
    h4 = pick([-1.0, -1.0, -1.0, -m1, -m2, -m3])
    h5 = pick([1.0, 1.0, 1.0, g1, g2, g3])
    e_cols = jnp.concatenate(
        [jnp.where(is_r, 0.0, h1), jnp.where(is_r, 0.0, h1), jnp.where(is_r, 0.0, h3), h4, zero, zero], axis=0
    )
    r_cols = jnp.concatenate(
        [jnp.where(is_r, h1, 0.0), jnp.where(is_r, h1, 0.0), jnp.where(is_r, h3, 0.0), zero, h5, zero], axis=0
    )
    right = jnp.concatenate([e_cols, r_cols], axis=1).astype(BF16)
    pair = dot_tn(left, right)
    weight = jnp.where(mask != 0, jnp.exp2(pair[:, :128] / pair[:, 128:]), 0.0)
    wh, wl = split2(weight)
    top_o = jnp.where(sub == 7, occupied, top)
    stacked = jnp.concatenate([top_o, s[8:16]], axis=0)
    sh, sl = split2(stacked)
    lhs = jnp.concatenate(
        [jnp.concatenate([sh, sh], axis=1), jnp.concatenate([sl, jnp.zeros_like(sl)], axis=1)], axis=0
    )
    mixed = dot_nt(lhs, jnp.concatenate([wh, wl], axis=1))
    mixed = mixed[0:16] + mixed[16:32]
    ws = mixed[7:8]
    diff = top * ws - mixed[0:8]
    c1 = jnp.where(sub == 3, -0.03, 0.05)
    c2 = jnp.where(sub == 3, 0.0, 0.02)
    spin = s[8:16] - 0.01 * (s[8:16] * ws + mixed[8:16])
    return jnp.where(first, c1 * diff - c2 * pltpu.roll(diff, 4, 0), pltpu.roll(spin, 4, 0))


def contact_kernel(
    out_ref, mask_hbm, ret_ref,
    got_ref, res_ref, mask_ref, send_sem, got_sem, back_sem, ret_sem, mask_sem,
):
    me = lax.axis_index("gx") * 32 + lax.axis_index("gy")

    def mask_copy(i):
        part = pl.ds(16 * i, 16)
        return pltpu.make_async_copy(mask_hbm.at[part], mask_ref.at[part], mask_sem.at[i])

    for i in range(8):
        mask_copy(i).start()
    barrier = pltpu.get_barrier_semaphore()

    def signal(d, carry):
        pl.semaphore_signal(barrier, inc=1, device_id=lax.rem(me + d, DEV), device_id_type=LOGICAL)
        return carry

    lax.fori_loop(1, DEV, signal, 0)
    pl.semaphore_wait(barrier, DEV - 1)

    def send(d):
        peer = lax.rem(me + d, DEV)
        return pltpu.make_async_remote_copy(
            out_ref.at[peer, pl.ds(0, 11)], got_ref.at[me, pl.ds(0, 11)],
            send_sem.at[d], got_sem.at[me], device_id=peer, device_id_type=LOGICAL,
        )

    def got(d):
        peer = lax.rem(me + DEV - d, DEV)
        return pltpu.make_async_remote_copy(
            out_ref.at[peer, pl.ds(0, 11)], got_ref.at[peer, pl.ds(0, 11)],
            send_sem.at[d], got_sem.at[peer], device_id=peer, device_id_type=LOGICAL,
        )

    def back(d):
        peer = lax.rem(me + DEV - d, DEV)
        return pltpu.make_async_remote_copy(
            res_ref.at[peer, pl.ds(0, 7)], ret_ref.at[me, pl.ds(0, 7)],
            back_sem.at[d], ret_sem.at[me], device_id=peer, device_id_type=LOGICAL,
        )

    def returned(d):
        peer = lax.rem(me + d, DEV)
        return pltpu.make_async_remote_copy(
            res_ref.at[peer, pl.ds(0, 7)], ret_ref.at[peer, pl.ds(0, 7)],
            back_sem.at[d], ret_sem.at[peer], device_id=peer, device_id_type=LOGICAL,
        )

    def start_send(d, carry):
        send(d).start()
        return carry

    lax.fori_loop(1, DEV, start_send, 0)
    for i in range(8):
        mask_copy(i).wait()
    tail = jnp.zeros((5, 128), F32)
    ret_ref[me] = contact_block(out_ref[me], mask_ref[me])

    def step(d, carry):
        peer = lax.rem(me + DEV - d, DEV)
        got(d).wait_recv()
        s = jnp.concatenate([got_ref[peer, 0:11, :], tail], axis=0)
        res_ref[peer] = contact_block(s, mask_ref[peer])

        @pl.when(d > 1)
        def _():
            back(d - 1).start()

        return carry

    lax.fori_loop(1, DEV, step, 0)
    back(DEV - 1).start()

    def finish(d, carry):
        send(d).wait_send()
        back(d).wait_send()
        returned(d).wait_recv()
        return carry

    lax.fori_loop(1, DEV, finish, 0)


def exchange(outgoing, mask):
    return pl.pallas_call(
        contact_kernel,
        out_shape=jax.ShapeDtypeStruct((DEV, 8, 128), F32),
        in_specs=[pl.BlockSpec(memory_space=VMEM), pl.BlockSpec(memory_space=pl.ANY)],
        out_specs=pl.BlockSpec(memory_space=VMEM),
        scratch_shapes=[
            VMEM((DEV, 16, 128), F32),
            VMEM((DEV, 8, 128), F32),
            VMEM((DEV, 128, 128), I32),
            pltpu.SemaphoreType.DMA((DEV,)),
            pltpu.SemaphoreType.DMA((DEV,)),
            pltpu.SemaphoreType.DMA((DEV,)),
            pltpu.SemaphoreType.DMA((DEV,)),
            pltpu.SemaphoreType.DMA((8,)),
        ],
        compiler_params=pltpu.CompilerParams(collective_id=0, has_side_effects=True),
        name="exchange",
    )(outgoing, mask)


def gather_kernel(field_ref, cell_ref, seen_ref, f_ref):
    for c in range(4):
        ft = jnp.transpose(field_ref[c])
        hi, lo = split2(ft)
        f_ref[pl.ds(128 * c, 128), 0:256] = hi
        f_ref[pl.ds(128 * c, 128), 256:512] = lo

    def step(k, carry):
        cell = row2(cell_ref, k)
        high = hot(iota((256, PB), 0) == (cell >> 7))
        part = dot_nn(f_ref[...], jnp.concatenate([high, high], axis=0))
        low = iota((128, PB), 0) == (cell & 127)
        rows = [
            jnp.sum(jnp.where(low, part[128 * c : 128 * c + 128], 0.0), axis=0, keepdims=True)
            for c in range(4)
        ]
        seen_ref[:, pl.ds(pl.multiple_of(k * PB, PB), PB)] = jnp.concatenate(rows, axis=0)
        return carry

    lax.fori_loop(0, NBLK, step, 0)


def gather(field, cell):
    return pl.pallas_call(
        gather_kernel,
        out_shape=jax.ShapeDtypeStruct((4, PARTS), F32),
        in_specs=[pl.BlockSpec(memory_space=VMEM)] * 2,
        out_specs=pl.BlockSpec(memory_space=VMEM),
        scratch_shapes=[VMEM((512, 512), BF16)],
        name="gather",
    )(field, cell)


def finish_kernel(
    owner_ref, sc_ref, q_ref, cell_ref, ret_ref, seen_ref, mot_ref, rad_ref, tmp_ref,
    next_ref, dep_ref,
    dense_ref, left_ref, acc_ref,
):
    lane = iota((8, 128), 1)

    def pack(b, carry):
        start = sc_ref[0, b]
        tile, off = start >> 7, start & 127
        mine = pltpu.roll(ret_ref[owner_ref[b]], off, 1)
        dense_ref[tile] = jnp.where(lane < off, dense_ref[tile], mine)
        dense_ref[tile + 1] = mine
        return carry

    lax.fori_loop(0, DEV, pack, 0, unroll=2)
    hi, lo = split2(dense_ref[0:64].reshape(512, 128))
    left_ref[:, 0:128] = hi
    left_ref[:, 128:256] = lo
    acc_ref[...] = jnp.zeros_like(acc_ref)

    def step(k, carry):
        lanes = pl.ds(pl.multiple_of(k * PB, PB), PB)
        q = row2(q_ref, k)
        low = hot(iota((128, PB), 0) == (q & 127))
        part = dot_nn(left_ref[...], jnp.concatenate([low, low], axis=0))
        high = jnp.broadcast_to(q >> 7, (8, PB))
        res = part[0:8]
        for t in range(1, 64):
            res = jnp.where(high == t, part[8 * t : 8 * t + 8], res)
        r = row2(rad_ref, k)
        temp = row2(tmp_ref, k)
        u = seen_ref[0:3, lanes]
        gas = seen_ref[3:4, lanes]
        v = mot_ref[0:3, lanes]
        drag = 4.0 / (r * r + 0.25) * (u - v)
        vn = v + (res[0:3] + 0.1 * drag) - jnp.where(iota((3, PB), 0) == 2, 0.03, 0.0)
        tn = temp + (res[3:4] + 0.4 * (gas - temp))
        next_ref[0:3, lanes] = vn
        next_ref[3:6, lanes] = res[4:7]
        next_ref[6:7, lanes] = tn
        volume = r * r * r
        push = -volume * drag
        rows = [volume, push[0:1], push[1:2], push[2:3], volume * (tn - gas)]
        cell = row2(cell_ref, k)
        lo_hot = hot(iota((256, PB), 0) == (cell & 255))
        hi_hot = hot(iota((128, PB), 0) == (cell >> 8))
        his, los = [], []
        for x in rows:
            hi, lo = split2(jnp.broadcast_to(x, (128, PB)))
            his.append(hi * hi_hot)
            los.append(lo * hi_hot)
        left = jnp.concatenate(
            [jnp.concatenate(his, axis=0), jnp.concatenate(los, axis=0)], axis=1
        )
        add2(acc_ref, dot_nt(left, jnp.concatenate([lo_hot, lo_hot], axis=1)))
        return carry

    lax.fori_loop(0, NBLK, step, 0)
    for f in range(5):
        for j in range(2):
            dep_ref[f, pl.ds(j, 128, stride=2), :] = acc_ref[j, pl.ds(128 * f, 128), :]


def finish(owner, sc, q, cell, ret, seen, mot, rad, tmp):
    return pl.pallas_call(
        finish_kernel,
        out_shape=(
            jax.ShapeDtypeStruct((7, PARTS), F32),
            jax.ShapeDtypeStruct((5, 256, 128), F32),
        ),
        in_specs=[pl.BlockSpec(memory_space=pltpu.SMEM)] * 2 + [pl.BlockSpec(memory_space=VMEM)] * 7,
        out_specs=(pl.BlockSpec(memory_space=VMEM),) * 2,
        scratch_shapes=[
            VMEM((66, 8, 128), F32),
            VMEM((512, 256), BF16),
            VMEM((2, 640, 128), F32),
        ],
        name="finish",
    )(owner, sc, q, cell, ret, seen, mot, rad, tmp)


def with_halo(value, sides):
    edges = {}
    for axis, dim in sides:
        size, length = (lax.axis_size(axis), value.shape[dim])
        up = [(i, i + 1) for i in range(size - 1)]
        last = lax.slice_in_dim(value, length - 1, length, axis=dim)
        first = lax.slice_in_dim(value, 0, 1, axis=dim)
        edges[dim] = (
            lax.ppermute(last, axis, up),
            lax.ppermute(first, axis, [(b, a) for a, b in up]),
        )
    done = []
    for _, dim in sides:
        low, high = edges[dim]
        around = [(1, 1) if d in done else (0, 0) for d in range(value.ndim)]
        value = jnp.concatenate([jnp.pad(low, around), value, jnp.pad(high, around)], axis=dim)
        done.append(dim)
    return value


def stencil(padded):
    interior = padded[:, :, 1:-1, 1:-1]
    z_padded = jnp.pad(interior, ((0, 0), (1, 1), (0, 0), (0, 0)))
    beside_all = z_padded[:, 2:] + z_padded[:, :-2]
    beside_all = beside_all + padded[:, :, 2:, 1:-1] + padded[:, :, :-2, 1:-1]
    beside_all = beside_all + padded[:, :, 1:-1, 2:] + padded[:, :, 1:-1, :-2]
    return 0.25 * interior + 0.125 * beside_all


def shards(fluid, pos, mot, rad, tmp, cell, box, box_owner, mask):
    rad2, tmp2 = rad.reshape(64, 128), tmp.reshape(64, 128)
    cell2, box2 = cell.reshape(64, 128), box.reshape(64, 128)
    filtered = stencil(with_halo(fluid, (("gx", 3), ("gy", 2))))
    seen = gather(filtered.reshape(4, 256, 128), cell2)
    outgoing, q, sc = place(box_owner, box2, pos, mot, rad2, tmp2)
    ret = exchange(outgoing, mask)
    nxt, dep = finish(box_owner, sc, q, cell2, ret, seen, mot, rad2, tmp2)
    spread = stencil(with_halo(dep.reshape(5, 32, 8, 128), (("gx", 3), ("gy", 2))))
    crowding = 1.0 + 4.0 * spread[0]
    fluid_next = fluid + 0.4 * spread[1:5] * crowding
    return fluid_next, 1.0 / crowding, nxt


def solution(mesh):
    return jax.shard_map(
        shards,
        mesh=mesh,
        in_specs=(
            P(None, None, "gy", "gx"),
            P(None, GX_GY),
            P(None, GX_GY),
            P(GX_GY),
            P(GX_GY),
            P(GX_GY),
            P(GX_GY, None),
            P(),
            P(GX_GY, None, None),
        ),
        out_specs=(P(None, None, "gy", "gx"), P(None, "gy", "gx"), P(None, GX_GY)),
        check_vma=False,
    )
```

```python
import functools

import jax
import jax.numpy as jnp
from jax import lax
from jax.experimental import pallas as pl
from jax.experimental.pallas import tpu as pltpu
from jax.sharding import PartitionSpec as P

GX_GY = ("gx", "gy")
LOGICAL = pl.DeviceIdType.LOGICAL
F32, BF16, I32 = jnp.float32, jnp.bfloat16, jnp.int32
DEV = 128
PARTS = 8192
PB = 256
NBLK = PARTS // PB
LOG2E = 1.4426950408889634
VMEM = pltpu.VMEM


def iota(shape, dim):
    return lax.broadcasted_iota(I32, shape, dim)


def hot(mask):
    return jnp.where(mask, 1.0, 0.0).astype(BF16)


def split2(x):
    hi = x.astype(BF16)
    lo = (x - hi.astype(F32)).astype(BF16)
    return hi, lo


def dot_nt(a, b):
    return lax.dot_general(a, b, (((1,), (1,)), ((), ())), preferred_element_type=F32)


def dot_nn(a, b):
    return lax.dot_general(a, b, (((1,), (0,)), ((), ())), preferred_element_type=F32)


def dot_tn(a, b):
    return lax.dot_general(a, b, (((0,), (0,)), ((), ())), preferred_element_type=F32)


def row2(ref, k):
    return jnp.concatenate([ref[pl.ds(2 * k, 1), :], ref[pl.ds(2 * k + 1, 1), :]], axis=1)


def add2(ref, x):
    n = x.shape[0]
    ref[0, 0:n] += x[:, :128]
    ref[1, 0:n] += x[:, 128:]


def rank_and_sort(owner_ref, box_ref, pos_ref, mot_ref, rad_ref, tmp_ref, q_ref, sc_ref, rank_ref, acc_ref, sorted_ref, smem_ref, sem):
    tri = hot(iota((PB, PB), 0) < iota((PB, PB), 1))

    def rank_step(k, before):
        box = row2(box_ref, k)
        match = iota((DEV, PB), 0) == box
        within = dot_nn(hot(match), tri)
        rank = jnp.sum(jnp.where(match, within + before, 0.0), axis=0, keepdims=True)
        rank_ref[pl.ds(2 * k, 1), :] = rank[:, :128]
        rank_ref[pl.ds(2 * k + 1, 1), :] = rank[:, 128:]
        return before + jnp.sum(jnp.where(match, 1.0, 0.0), axis=1, keepdims=True)

    counts = lax.fori_loop(0, NBLK, rank_step, jnp.zeros((DEV, 1), F32))
    down, over = iota((DEV, DEV), 0), iota((DEV, DEV), 1)
    wide = jnp.broadcast_to(counts, (DEV, DEV))
    start_row = jnp.sum(jnp.where(down < over, wide, 0.0), axis=0, keepdims=True)
    start_col = jnp.sum(jnp.where(down == over, start_row, 0.0), axis=1, keepdims=True)
    owner_col = jnp.sum(jnp.where(down == over, owner_ref[0:1, :], 0), axis=1, keepdims=True)
    holds = owner_col == over
    start_at = jnp.sum(jnp.where(holds, start_col, 0.0), axis=0, keepdims=True)
    count_at = jnp.sum(jnp.where(holds, counts, 0.0), axis=0, keepdims=True)
    sub = iota((8, DEV), 0)
    sc_ref[...] = jnp.where(sub == 0, start_row, jnp.where(sub == 1, start_at, count_at)).astype(I32)
    copy = pltpu.make_async_copy(sc_ref, smem_ref, sem)
    copy.start()
    table = jnp.broadcast_to(start_row, (64, DEV))
    q = rank_ref[...] + jnp.take_along_axis(table, box_ref[...], axis=1)
    q_ref[...] = q.astype(I32)
    acc_ref[...] = jnp.zeros_like(acc_ref)

    def sort_step(k, carry):
        q = row2(q_ref, k)
        lo_hot = hot(iota((PB, PB), 0) == (q & 255))
        hi_hot = hot(iota((32, PB), 0) == (q >> 8))
        lanes = pl.ds(pl.multiple_of(k * PB, PB), PB)
        rows = [pos_ref[c : c + 1, lanes] for c in range(3)]
        rows += [row2(tmp_ref, k)]
        rows += [mot_ref[c : c + 1, lanes] for c in range(3)]
        rows += [row2(rad_ref, k)]
        rows += [mot_ref[c : c + 1, lanes] for c in range(3, 6)]
        left = spread_rows(rows, hi_hot, 32)
        add2(acc_ref, dot_nt(left, jnp.concatenate([lo_hot, lo_hot], axis=1)))
        return carry

    lax.fori_loop(0, NBLK, sort_step, 0)
    for t in range(64):
        sorted_ref[t, 0:11, :] = acc_ref[t % 2, pl.ds(t // 2, 11, stride=32), :]
    copy.wait()


def spread_rows(rows, hi_hot, n):
    his, los = [], []
    for x in rows:
        hi, lo = split2(jnp.broadcast_to(x, (n, PB)))
        his.append(hi * hi_hot)
        los.append(lo * hi_hot)
    return jnp.concatenate([jnp.concatenate(his, axis=0), jnp.concatenate(los, axis=0)], axis=1)


def windows(sorted_ref, smem_ref, out_ref):
    lane = iota((16, 128), 1)

    def window(o, carry):
        start = smem_ref[1, o]
        count = smem_ref[2, o]
        tile, off = jnp.clip(start >> 7, 0, 64), start & 127
        shift = (128 - off) & 127
        low = pltpu.roll(sorted_ref[tile], shift, 1)
        high = pltpu.roll(sorted_ref[tile + 1], shift, 1)
        both = jnp.where(lane < 128 - off, low, high)
        out_ref[o] = jnp.where(lane < count, both, 0.0)
        return carry

    lax.fori_loop(0, DEV, window, 0, unroll=8)


def contact_block(s, mask):
    sub = iota((8, 128), 0)
    top = s[0:8]
    r = s[7:8]
    occupied = jnp.where(r > 0.0, 1.0, 0.0)
    scale = jnp.where((sub & 3) == 3, 1.4142135623730951, (2.0 * LOG2E) ** 0.5)
    pos4 = jnp.concatenate([s[0:3], r, s[0:3], r], axis=0)
    y = pos4 * scale
    a = y.astype(BF16).astype(F32)
    b = (y - a).astype(BF16).astype(F32)
    c = y - a - b
    first = sub < 4
    is_r = (sub & 3) == 3
    sq = y * y * 0.5
    m = jnp.sum(jnp.where(first & ~is_r, sq, 0.0), axis=0, keepdims=True)
    g = sq[3:4] + 0.5

    def three(v):
        v1 = v.astype(BF16).astype(F32)
        v2 = (v - v1).astype(BF16).astype(F32)
        return v1, v2, v - v1 - v2

    m1, m2, m3 = three(m)
    g1, g2, g3 = three(g)

    def pick(rows):
        out = jnp.zeros((8, 128), F32)
        for i, v in enumerate(rows):
            out = jnp.where(sub == i, v, out)
        return out

    zero = jnp.zeros((8, 128), F32)
    left = jnp.concatenate(
        [a, b, jnp.where(first, a, c), pick([m1, m2, m3, 1.0, 1.0, 1.0]), pick([g1, g2, g3, 1.0, 1.0, 1.0]), zero], axis=0
    ).astype(BF16)
    h1 = jnp.where(first, a, b)
    h3 = jnp.where(first, c, a)
    h4 = pick([-1.0, -1.0, -1.0, -m1, -m2, -m3])
    h5 = pick([1.0, 1.0, 1.0, g1, g2, g3])
    e_cols = jnp.concatenate(
        [jnp.where(is_r, 0.0, h1), jnp.where(is_r, 0.0, h1), jnp.where(is_r, 0.0, h3), h4, zero, zero], axis=0
    )
    r_cols = jnp.concatenate(
        [jnp.where(is_r, h1, 0.0), jnp.where(is_r, h1, 0.0), jnp.where(is_r, h3, 0.0), zero, h5, zero], axis=0
    )
    right = jnp.concatenate([e_cols, r_cols], axis=1).astype(BF16)
    pair = dot_tn(left, right)
    weight = jnp.where(mask != 0, jnp.exp2(pair[:, :128] / pair[:, 128:]), 0.0)
    wh, wl = split2(weight)
    top_o = jnp.where(sub == 7, occupied, top)
    stacked = jnp.concatenate([top_o, s[8:16]], axis=0)
    sh, sl = split2(stacked)
    lhs = jnp.concatenate(
        [jnp.concatenate([sh, sh], axis=1), jnp.concatenate([sl, jnp.zeros_like(sl)], axis=1)], axis=0
    )
    mixed = dot_nt(lhs, jnp.concatenate([wh, wl], axis=1))
    mixed = mixed[0:16] + mixed[16:32]
    ws = mixed[7:8]
    diff = top * ws - mixed[0:8]
    c1 = jnp.where(sub == 3, -0.03, 0.05)
    c2 = jnp.where(sub == 3, 0.0, 0.02)
    spin = s[8:16] - 0.01 * (s[8:16] * ws + mixed[8:16])
    return jnp.where(first, c1 * diff - c2 * pltpu.roll(diff, 4, 0), pltpu.roll(spin, 4, 0))


def edges(src_ref, n, ylow_ref, yhigh_ref, xlow_ref, xhigh_ref):
    lane = iota((8, 128), 1)
    first = jnp.zeros((8, 128), F32)
    last = jnp.zeros((8, 128), F32)
    for j in range(n * 32):
        v = src_ref[8 * j : 8 * j + 8, :]
        ylow_ref[j : j + 1, :] = v[0:1]
        yhigh_ref[j : j + 1, :] = v[7:8]
        first = jnp.where(lane == j, pltpu.roll(v, j, 1), first)
        last = jnp.where(lane == j, pltpu.roll(v, (j + 1) % 128, 1), last)
    xlow_ref[...] = first
    xhigh_ref[...] = last


def neighbours():
    ix, iy = lax.axis_index("gx"), lax.axis_index("gy")
    up_x = lax.rem(ix + 1, 4) * 32 + iy
    down_x = lax.rem(ix + 3, 4) * 32 + iy
    up_y = ix * 32 + lax.rem(iy + 1, 32)
    down_y = ix * 32 + lax.rem(iy + 31, 32)
    return down_y, up_y, down_x, up_x


def halo_copies(mine, theirs, send_sem, recv_sem):
    down_y, up_y, down_x, up_x = neighbours()
    plan = ((0, 1, down_y), (1, 0, up_y), (2, 3, down_x), (3, 2, up_x))
    return [
        pltpu.make_async_remote_copy(
            mine[a], theirs[b], send_sem.at[a], recv_sem.at[b], device_id=dev, device_id_type=LOGICAL
        )
        for a, b, dev in plan
    ]


def smooth(src_ref, n, halo, out_ref):
    ylo, yhi, xlo_ref, xhi_ref = halo
    ix, iy = lax.axis_index("gx"), lax.axis_index("gy")
    sub, lane = iota((8, 128), 0), iota((8, 128), 1)
    xlo = jnp.where(ix > 0, xlo_ref[...], 0.0)
    xhi = jnp.where(ix < 3, xhi_ref[...], 0.0)
    zero = jnp.zeros((8, 128), F32)
    for f in range(n):
        for z in range(32):
            j = f * 32 + z
            at = lambda i: src_ref[8 * i : 8 * i + 8, :]
            c = at(j)
            total = (at(j - 1) if z > 0 else zero) + (at(j + 1) if z < 31 else zero)
            low = jnp.where(iy > 0, ylo[j : j + 1, :], 0.0)
            high = jnp.where(iy < 31, yhi[j : j + 1, :], 0.0)
            total += jnp.where(sub == 0, low, pltpu.roll(c, 1, 0))
            total += jnp.where(sub == 7, high, pltpu.roll(c, 7, 0))
            total += jnp.where(lane == 0, pltpu.roll(xlo, (128 - j) % 128, 1), pltpu.roll(c, 1, 1))
            total += jnp.where(lane == 127, pltpu.roll(xhi, (255 - j) % 128, 1), pltpu.roll(c, 127, 1))
            out_ref[8 * j : 8 * j + 8, :] = 0.25 * c + 0.125 * total


def gather(field_ref, cell_ref, seen_ref, f_ref):
    for c in range(4):
        hi, lo = split2(jnp.transpose(field_ref[256 * c : 256 * c + 256, :]))
        f_ref[pl.ds(128 * c, 128), 0:256] = hi
        f_ref[pl.ds(128 * c, 128), 256:512] = lo

    def step(k, carry):
        cell = row2(cell_ref, k)
        high = hot(iota((256, PB), 0) == (cell >> 7))
        part = dot_nn(f_ref[...], jnp.concatenate([high, high], axis=0))
        low = iota((128, PB), 0) == (cell & 127)
        rows = [
            jnp.sum(jnp.where(low, part[128 * c : 128 * c + 128], 0.0), axis=0, keepdims=True)
            for c in range(4)
        ]
        seen_ref[:, pl.ds(pl.multiple_of(k * PB, PB), PB)] = jnp.concatenate(rows, axis=0)
        return carry

    lax.fori_loop(0, NBLK, step, 0)


def deposit_block(rows, cell, acc_ref):
    lo_hot = hot(iota((256, PB), 0) == (cell & 255))
    hi_hot = hot(iota((128, PB), 0) == (cell >> 8))
    left = spread_rows(rows, hi_hot, 128)
    add2(acc_ref, dot_nt(left, jnp.concatenate([lo_hot, lo_hot], axis=1)))


def unfold(acc_ref, n, dep_ref):
    for j in range(2):
        dep_ref[pl.ds(j, n * 128, stride=2), :] = acc_ref[j]


def drag_of(seen_ref, mot_ref, r, lanes):
    return 4.0 / (r * r + 0.25) * (seen_ref[0:3, lanes] - mot_ref[0:3, lanes])


GROUP = 8


def main_kernel(
    owner_ref, box_ref, pos_ref, mot_ref, rad_ref, tmp_ref, cell_ref, fluid_ref, mask_hbm,
    ret_ref, q_ref, sc_ref, seen_ref, spread_ref,
    rank_ref, acc_ref, sorted_ref, smem_ref, out_ref, got_ref, res_ref, mask_ref,
    field_ref, f_ref, dacc_ref, dep_ref,
    ey0, ey1, ex0, ex1, hy0, hy1, hx0, hx1,
    gy0, gy1, gx0, gx1, ky0, ky1, kx0, kx1,
    table_sem, send_sem, got_sem, back_sem, ret_sem, mask_sem, hs_sem, hr_sem, ks_sem, kr_sem,
):
    me = lax.axis_index("gx") * 32 + lax.axis_index("gy")
    got_ref[...] = jnp.zeros_like(got_ref)
    barrier = pltpu.get_barrier_semaphore()

    def signal(d, carry):
        pl.semaphore_signal(barrier, inc=1, device_id=lax.rem(me + d, DEV), device_id_type=LOGICAL)
        return carry

    lax.fori_loop(1, DEV, signal, 0)

    def mask_copy(i):
        part = pl.ds(16 * i, 16)
        return pltpu.make_async_copy(mask_hbm.at[part], mask_ref.at[part], mask_sem.at[i])

    for i in range(8):
        mask_copy(i).start()
    edges(fluid_ref, 4, ey0, ey1, ex0, ex1)
    rank_and_sort(owner_ref, box_ref, pos_ref, mot_ref, rad_ref, tmp_ref, q_ref, sc_ref, rank_ref, acc_ref, sorted_ref, smem_ref, table_sem)
    windows(sorted_ref, smem_ref, out_ref)
    pl.semaphore_wait(barrier, DEV - 1)
    fluid_halo = halo_copies((ey0, ey1, ex0, ex1), (hy0, hy1, hx0, hx1), hs_sem, hr_sem)
    for copy in fluid_halo:
        copy.start()

    def send(d):
        peer = lax.rem(me + d, DEV)
        return pltpu.make_async_remote_copy(
            out_ref.at[peer, pl.ds(0, 11)], got_ref.at[me, pl.ds(0, 11)],
            send_sem.at[d], got_sem.at[me], device_id=peer, device_id_type=LOGICAL,
        )

    def got(d):
        peer = lax.rem(me + DEV - d, DEV)
        return pltpu.make_async_remote_copy(
            out_ref.at[peer, pl.ds(0, 11)], got_ref.at[peer, pl.ds(0, 11)],
            send_sem.at[d], got_sem.at[peer], device_id=peer, device_id_type=LOGICAL,
        )

    def back(d):
        peer = lax.rem(me + DEV - d, DEV)
        return pltpu.make_async_remote_copy(
            res_ref.at[peer, pl.ds(0, 7)], ret_ref.at[me, pl.ds(0, 7)],
            back_sem.at[d], ret_sem.at[me], device_id=peer, device_id_type=LOGICAL,
        )

    def returned(d):
        peer = lax.rem(me + d, DEV)
        return pltpu.make_async_remote_copy(
            res_ref.at[peer, pl.ds(0, 7)], ret_ref.at[peer, pl.ds(0, 7)],
            back_sem.at[d], ret_sem.at[peer], device_id=peer, device_id_type=LOGICAL,
        )

    def start_send(d, carry):
        send(d).start()
        return carry

    lax.fori_loop(1, DEV, start_send, 0)
    got_ref[me] = out_ref[me]
    for copy in fluid_halo:
        copy.wait()
    smooth(fluid_ref, 4, (hy0, hy1, hx0, hx1), field_ref)
    gather(field_ref, cell_ref, seen_ref, f_ref)
    for i in range(8):
        mask_copy(i).wait()

    def contacts(first):
        peers = [lax.rem(me + DEV - (first + k), DEV) for k in range(GROUP)]
        given = [got_ref[p] for p in peers]
        results = [contact_block(s, mask_ref[p]) for s, p in zip(given, peers)]
        for p, r in zip(peers, results):
            res_ref[p] = r

    def await_group(first, skip):
        for k in range(skip, GROUP):
            got(first + k).wait_recv()

    def send_back(first, skip):
        for k in range(skip, GROUP):
            back(first + k).start()

    await_group(0, 1)
    contacts(0)
    await_group(GROUP, 0)
    contacts(GROUP)
    send_back(0, 1)

    def group(g, carry):
        await_group(g * GROUP, 0)
        contacts(g * GROUP)
        send_back(g * GROUP - GROUP, 0)
        return carry

    lax.fori_loop(2, DEV // GROUP, group, 0)
    for k in range(GROUP):
        back(DEV - GROUP + k).start()
    ret_ref[me] = res_ref[me]

    dacc_ref[...] = jnp.zeros_like(dacc_ref)

    def deposit(k, carry):
        lanes = pl.ds(pl.multiple_of(k * PB, PB), PB)
        r = row2(rad_ref, k)
        volume = r * r * r
        push = -volume * drag_of(seen_ref, mot_ref, r, lanes)
        deposit_block([volume, push[0:1], push[1:2], push[2:3]], row2(cell_ref, k), dacc_ref)
        return carry

    lax.fori_loop(0, NBLK, deposit, 0)
    unfold(dacc_ref, 4, dep_ref)
    edges(dep_ref, 4, gy0, gy1, gx0, gx1)
    dep_halo = halo_copies((gy0, gy1, gx0, gx1), (ky0, ky1, kx0, kx1), ks_sem, kr_sem)
    for copy in dep_halo:
        copy.start()

    def close(d, carry):
        send(d).wait_send()
        back(d).wait_send()
        returned(d).wait_recv()
        return carry

    lax.fori_loop(1, DEV, close, 0)
    for copy in dep_halo:
        copy.wait()
    smooth(dep_ref, 4, (ky0, ky1, kx0, kx1), spread_ref)


def halo_scratch(n):
    return [VMEM((n * 32, 128), F32), VMEM((n * 32, 128), F32), VMEM((8, 128), F32), VMEM((8, 128), F32)]


def vmem_specs(n):
    return [pl.BlockSpec(memory_space=VMEM)] * n


def main(owner, box, pos, mot, rad, tmp, cell, fluid, mask):
    dma = pltpu.SemaphoreType.DMA
    return pl.pallas_call(
        main_kernel,
        out_shape=(
            jax.ShapeDtypeStruct((DEV, 8, 128), F32),
            jax.ShapeDtypeStruct((64, 128), I32),
            jax.ShapeDtypeStruct((8, 128), I32),
            jax.ShapeDtypeStruct((4, PARTS), F32),
            jax.ShapeDtypeStruct((1024, 128), F32),
        ),
        in_specs=vmem_specs(8) + [pl.BlockSpec(memory_space=pl.ANY)],
        out_specs=tuple(vmem_specs(5)),
        scratch_shapes=[
            VMEM((64, 128), F32),
            VMEM((2, 384, 128), F32),
            VMEM((66, 16, 128), F32),
            pltpu.SMEM((8, 128), I32),
            VMEM((DEV, 16, 128), F32),
            VMEM((DEV, 16, 128), F32),
            VMEM((DEV, 8, 128), F32),
            VMEM((DEV, 128, 128), I32),
            VMEM((1024, 128), F32),
            VMEM((512, 512), BF16),
            VMEM((2, 512, 128), F32),
            VMEM((1032, 128), F32),
            *halo_scratch(4), *halo_scratch(4), *halo_scratch(4), *halo_scratch(4),
            dma, dma((DEV,)), dma((DEV,)), dma((DEV,)), dma((DEV,)), dma((8,)),
            dma((4,)), dma((4,)), dma((4,)), dma((4,)),
        ],
        compiler_params=pltpu.CompilerParams(collective_id=0, has_side_effects=True),
        name="main",
    )(owner, box, pos, mot, rad, tmp, cell, fluid, mask)


def fetch_kernel(
    owner_ref, sc_ref, q_ref, cell_ref, ret_ref, seen_ref, mot_ref, rad_ref, tmp_ref,
    next_ref, dep_ref,
    dense_ref, left_ref, acc_ref,
):
    lane = iota((8, 128), 1)

    def pack(b, carry):
        start = sc_ref[0, b]
        tile, off = jnp.clip(start >> 7, 0, 64), start & 127
        mine = pltpu.roll(ret_ref[owner_ref[b]], off, 1)
        dense_ref[tile] = jnp.where(lane < off, dense_ref[tile], mine)
        dense_ref[tile + 1] = mine
        return carry

    lax.fori_loop(0, DEV, pack, 0, unroll=2)
    hi, lo = split2(dense_ref[0:64].reshape(512, 128))
    left_ref[:, 0:128] = hi
    left_ref[:, 128:256] = lo
    acc_ref[...] = jnp.zeros_like(acc_ref)

    def step(k, carry):
        lanes = pl.ds(pl.multiple_of(k * PB, PB), PB)
        q = row2(q_ref, k)
        low = hot(iota((128, PB), 0) == (q & 127))
        part = dot_nn(left_ref[...], jnp.concatenate([low, low], axis=0))
        high = jnp.broadcast_to(q >> 7, (8, PB))
        res = part[0:8]
        for t in range(1, 64):
            res = jnp.where(high == t, part[8 * t : 8 * t + 8], res)
        r = row2(rad_ref, k)
        temp = row2(tmp_ref, k)
        gas = seen_ref[3:4, lanes]
        drag = drag_of(seen_ref, mot_ref, r, lanes)
        vn = mot_ref[0:3, lanes] + (res[0:3] + 0.1 * drag) - jnp.where(iota((3, PB), 0) == 2, 0.03, 0.0)
        tn = temp + (res[3:4] + 0.4 * (gas - temp))
        next_ref[0:3, lanes] = vn
        next_ref[3:6, lanes] = res[4:7]
        next_ref[6:7, lanes] = tn
        deposit_block([r * r * r * (tn - gas)], row2(cell_ref, k), acc_ref)
        return carry

    lax.fori_loop(0, NBLK, step, 0)
    unfold(acc_ref, 1, dep_ref)


def fetch(owner, sc, q, cell, ret, seen, mot, rad, tmp):
    return pl.pallas_call(
        fetch_kernel,
        out_shape=(jax.ShapeDtypeStruct((7, PARTS), F32), jax.ShapeDtypeStruct((264, 128), F32)),
        in_specs=[pl.BlockSpec(memory_space=pltpu.SMEM)] * 2 + vmem_specs(7),
        out_specs=tuple(vmem_specs(2)),
        scratch_shapes=[VMEM((66, 8, 128), F32), VMEM((512, 256), BF16), VMEM((2, 128, 128), F32)],
        name="fetch",
    )(owner, sc, q, cell, ret, seen, mot, rad, tmp)


def end_kernel(
    dep_ref, spread_ref, fluid_ref, next_ref, void_ref,
    heat_ref, ey0, ey1, ex0, ex1, hy0, hy1, hx0, hx1, hs_sem, hr_sem,
):
    barrier = pltpu.get_barrier_semaphore()
    for dev in neighbours():
        pl.semaphore_signal(barrier, inc=1, device_id=dev, device_id_type=LOGICAL)
    edges(dep_ref, 1, ey0, ey1, ex0, ex1)
    crowding = 1.0 + 4.0 * spread_ref[0:256, :]
    void_ref[...] = 1.0 / crowding
    scale = 0.4 * crowding
    pl.semaphore_wait(barrier, 4)
    halo = halo_copies((ey0, ey1, ex0, ex1), (hy0, hy1, hx0, hx1), hs_sem, hr_sem)
    for copy in halo:
        copy.start()
    for f in range(3):
        at = slice(256 * f, 256 * f + 256)
        next_ref[at, :] = fluid_ref[at, :] + spread_ref[256 * f + 256 : 256 * f + 512, :] * scale
    for copy in halo:
        copy.wait()
    smooth(dep_ref, 1, (hy0, hy1, hx0, hx1), heat_ref)
    next_ref[768:1024, :] = fluid_ref[768:1024, :] + heat_ref[...] * scale


def end(dep, spread, fluid):
    dma = pltpu.SemaphoreType.DMA
    return pl.pallas_call(
        end_kernel,
        out_shape=(jax.ShapeDtypeStruct((1024, 128), F32), jax.ShapeDtypeStruct((256, 128), F32)),
        in_specs=vmem_specs(3),
        out_specs=tuple(vmem_specs(2)),
        scratch_shapes=[VMEM((256, 128), F32), *halo_scratch(1), *halo_scratch(1), dma((4,)), dma((4,))],
        compiler_params=pltpu.CompilerParams(collective_id=1, has_side_effects=True),
        name="end",
    )(dep, spread, fluid)


def shards(fluid, pos, mot, rad, tmp, cell, box, box_owner, mask):
    rad2, tmp2 = rad.reshape(64, 128), tmp.reshape(64, 128)
    cell2, box2 = cell.reshape(64, 128), box.reshape(64, 128)
    fluid2 = fluid.reshape(1024, 128)
    ret, q, sc, seen, spread = main(box_owner.reshape(1, 128), box2, pos, mot, rad2, tmp2, cell2, fluid2, mask)
    nxt, dep = fetch(box_owner, sc, q, cell2, ret, seen, mot, rad2, tmp2)
    fluid_next, void = end(dep, spread, fluid2)
    return fluid_next.reshape(4, 32, 8, 128), void.reshape(32, 8, 128), nxt


def solution(mesh):
    return jax.shard_map(
        shards,
        mesh=mesh,
        in_specs=(
            P(None, None, "gy", "gx"),
            P(None, GX_GY),
            P(None, GX_GY),
            P(GX_GY),
            P(GX_GY),
            P(GX_GY),
            P(GX_GY, None),
            P(),
            P(GX_GY, None, None),
        ),
        out_specs=(P(None, None, "gy", "gx"), P(None, "gy", "gx"), P(None, GX_GY)),
        check_vma=False,
    )
```

```python
import functools

import jax
import jax.numpy as jnp
from jax import lax
from jax.experimental import pallas as pl
from jax.experimental.pallas import tpu as pltpu
from jax.sharding import PartitionSpec as P

GX_GY = ("gx", "gy")
LOGICAL = pl.DeviceIdType.LOGICAL
F32, BF16, I32 = jnp.float32, jnp.bfloat16, jnp.int32
DEV = 128
PARTS = 8192
RB = 256
PB = 2048
NBLK = PARTS // PB
LOG2E = 1.4426950408889634
VMEM = pltpu.VMEM


def iota(shape, dim):
    return lax.broadcasted_iota(I32, shape, dim)


def hot(mask):
    return jnp.where(mask, 1.0, 0.0).astype(BF16)


def split2(x):
    hi = x.astype(BF16)
    lo = (x - hi.astype(F32)).astype(BF16)
    return hi, lo


def dot_nt(a, b):
    return lax.dot_general(a, b, (((1,), (1,)), ((), ())), preferred_element_type=F32)


def dot_nn(a, b):
    return lax.dot_general(a, b, (((1,), (0,)), ((), ())), preferred_element_type=F32)


def dot_tn(a, b):
    return lax.dot_general(a, b, (((0,), (0,)), ((), ())), preferred_element_type=F32)


def row2(ref, k, size=PB):
    n = size // 128
    return jnp.concatenate([ref[pl.ds(n * k + i, 1), :] for i in range(n)], axis=1)


def add2(ref, x):
    n = x.shape[0] // 2
    x = x[:n] + x[n:]
    ref[0, 0:n] += x[:, :128]
    ref[1, 0:n] += x[:, 128:]


def rank_and_sort(signal, owner_ref, box_ref, pos_ref, mot_ref, rad_ref, tmp_ref, q_ref, sc_ref, rank_ref, acc_ref, sorted_ref, smem_ref, sem):
    tri = hot(iota((RB, RB), 0) < iota((RB, RB), 1))

    def rank_step(k, before):
        signal(k)
        box = row2(box_ref, k, RB)
        match = iota((DEV, RB), 0) == box
        within = dot_nn(hot(match), tri)
        rank = jnp.sum(jnp.where(match, within + before, 0.0), axis=0, keepdims=True)
        rank_ref[pl.ds(2 * k, 1), :] = rank[:, :128]
        rank_ref[pl.ds(2 * k + 1, 1), :] = rank[:, 128:]
        return before + jnp.sum(jnp.where(match, 1.0, 0.0), axis=1, keepdims=True)

    counts = lax.fori_loop(0, PARTS // RB, rank_step, jnp.zeros((DEV, 1), F32), unroll=8)
    down, over = iota((DEV, DEV), 0), iota((DEV, DEV), 1)
    wide = jnp.broadcast_to(counts, (DEV, DEV))
    start_row = jnp.sum(jnp.where(down < over, wide, 0.0), axis=0, keepdims=True)
    start_col = jnp.sum(jnp.where(down == over, start_row, 0.0), axis=1, keepdims=True)
    owner_col = jnp.sum(jnp.where(down == over, owner_ref[0:1, :], 0), axis=1, keepdims=True)
    holds = owner_col == over
    start_at = jnp.sum(jnp.where(holds, start_col, 0.0), axis=0, keepdims=True)
    count_at = jnp.sum(jnp.where(holds, counts, 0.0), axis=0, keepdims=True)
    sub = iota((8, DEV), 0)
    sc_ref[...] = jnp.where(sub == 0, start_row, jnp.where(sub == 1, start_at, count_at)).astype(I32)
    copy = pltpu.make_async_copy(sc_ref, smem_ref, sem)
    copy.start()
    table = jnp.broadcast_to(start_row, (64, DEV))
    q = rank_ref[...] + jnp.take_along_axis(table, box_ref[...], axis=1)
    q_ref[...] = q.astype(I32)
    acc_ref[...] = jnp.zeros_like(acc_ref)

    def sort_step(k, carry):
        q = row2(q_ref, k)
        lo_hot = hot(iota((256, PB), 0) == (q & 255))
        hi_hot = hot(iota((32, PB), 0) == (q >> 8))
        lanes = pl.ds(pl.multiple_of(k * PB, PB), PB)
        rows = [pos_ref[c : c + 1, lanes] for c in range(3)]
        rows += [row2(tmp_ref, k)]
        rows += [mot_ref[c : c + 1, lanes] for c in range(3)]
        rows += [row2(rad_ref, k)]
        rows += [mot_ref[c : c + 1, lanes] for c in range(3, 6)]
        left = spread_rows(rows, hi_hot, 32)
        add2(acc_ref, dot_nt(left, lo_hot))
        return carry

    lax.fori_loop(0, NBLK, sort_step, 0)
    for t in range(64):
        sorted_ref[t, 0:11, :] = acc_ref[t % 2, pl.ds(t // 2, 11, stride=32), :]
    copy.wait()


def spread_rows(rows, hi_hot, n):
    his, los = [], []
    for x in rows:
        hi, lo = split2(jnp.broadcast_to(x, (n, PB)))
        his.append(hi * hi_hot)
        los.append(lo * hi_hot)
    return jnp.concatenate(his + los, axis=0)


def window(sorted_ref, smem_ref, o):
    lane = iota((16, 128), 1)
    start = smem_ref[1, o]
    count = smem_ref[2, o]
    tile, off = jnp.clip(start >> 7, 0, 64), start & 127
    shift = (128 - off) & 127
    low = pltpu.roll(sorted_ref[tile], shift, 1)
    high = pltpu.roll(sorted_ref[tile + 1], shift, 1)
    both = jnp.where(lane < 128 - off, low, high)
    return jnp.where(lane < count, both, 0.0)


def contact_block(s, mask):
    sub = iota((8, 128), 0)
    top = s[0:8]
    r = s[7:8]
    occupied = jnp.where(r > 0.0, 1.0, 0.0)
    scale = jnp.where((sub & 3) == 3, 1.4142135623730951, (2.0 * LOG2E) ** 0.5)
    pos4 = jnp.concatenate([s[0:3], r, s[0:3], r], axis=0)
    y = pos4 * scale
    a = y.astype(BF16).astype(F32)
    b = (y - a).astype(BF16).astype(F32)
    c = y - a - b
    first = sub < 4
    is_r = (sub & 3) == 3
    sq = y * y * 0.5
    m = jnp.sum(jnp.where(first & ~is_r, sq, 0.0), axis=0, keepdims=True)
    g = sq[3:4] + 0.5

    def three(v):
        v1 = v.astype(BF16).astype(F32)
        v2 = (v - v1).astype(BF16).astype(F32)
        return v1, v2, v - v1 - v2

    m1, m2, m3 = three(m)
    g1, g2, g3 = three(g)

    def pick(rows):
        out = jnp.zeros((8, 128), F32)
        for i, v in enumerate(rows):
            out = jnp.where(sub == i, v, out)
        return out

    zero = jnp.zeros((8, 128), F32)
    left = jnp.concatenate(
        [a, b, jnp.where(first, a, c), pick([m1, m2, m3, 1.0, 1.0, 1.0]), pick([g1, g2, g3, 1.0, 1.0, 1.0]), zero], axis=0
    ).astype(BF16)
    h1 = jnp.where(first, a, b)
    h3 = jnp.where(first, c, a)
    h4 = pick([-1.0, -1.0, -1.0, -m1, -m2, -m3])
    h5 = pick([1.0, 1.0, 1.0, g1, g2, g3])
    e_cols = jnp.concatenate(
        [jnp.where(is_r, 0.0, h1), jnp.where(is_r, 0.0, h1), jnp.where(is_r, 0.0, h3), h4, zero, zero], axis=0
    )
    r_cols = jnp.concatenate(
        [jnp.where(is_r, h1, 0.0), jnp.where(is_r, h1, 0.0), jnp.where(is_r, h3, 0.0), zero, h5, zero], axis=0
    )
    right = jnp.concatenate([e_cols, r_cols], axis=1).astype(BF16)
    pair = dot_tn(left, right)
    weight = jnp.where(mask != 0, jnp.exp2(pair[:, :128] / pair[:, 128:]), 0.0)
    wh, wl = split2(weight)
    top_o = jnp.where(sub == 7, occupied, top)
    stacked = jnp.concatenate([top_o, s[8:16]], axis=0)
    sh, sl = split2(stacked)
    lhs = jnp.concatenate(
        [jnp.concatenate([sh, sh], axis=1), jnp.concatenate([sl, jnp.zeros_like(sl)], axis=1)], axis=0
    )
    mixed = dot_nt(lhs, jnp.concatenate([wh, wl], axis=1))
    mixed = mixed[0:16] + mixed[16:32]
    ws = mixed[7:8]
    diff = top * ws - mixed[0:8]
    c1 = jnp.where(sub == 3, -0.03, 0.05)
    c2 = jnp.where(sub == 3, 0.0, 0.02)
    spin = s[8:16] - 0.01 * (s[8:16] * ws + mixed[8:16])
    return jnp.where(first, c1 * diff - c2 * pltpu.roll(diff, 4, 0), pltpu.roll(spin, 4, 0))


def edges(src_ref, n, ylow_ref, yhigh_ref, xlow_ref, xhigh_ref):
    lane = iota((8, 128), 1)
    first = jnp.zeros((8, 128), F32)
    last = jnp.zeros((8, 128), F32)
    for j in range(n * 32):
        v = src_ref[8 * j : 8 * j + 8, :]
        ylow_ref[j : j + 1, :] = v[0:1]
        yhigh_ref[j : j + 1, :] = v[7:8]
        first = jnp.where(lane == j, pltpu.roll(v, j, 1), first)
        last = jnp.where(lane == j, pltpu.roll(v, (j + 1) % 128, 1), last)
    xlow_ref[...] = first
    xhigh_ref[...] = last


def neighbours():
    ix, iy = lax.axis_index("gx"), lax.axis_index("gy")
    up_x = lax.rem(ix + 1, 4) * 32 + iy
    down_x = lax.rem(ix + 3, 4) * 32 + iy
    up_y = ix * 32 + lax.rem(iy + 1, 32)
    down_y = ix * 32 + lax.rem(iy + 31, 32)
    return down_y, up_y, down_x, up_x


def halo_copies(mine, theirs, send_sem, recv_sem):
    down_y, up_y, down_x, up_x = neighbours()
    plan = ((0, 1, down_y), (1, 0, up_y), (2, 3, down_x), (3, 2, up_x))
    return [
        pltpu.make_async_remote_copy(
            mine[a], theirs[b], send_sem.at[a], recv_sem.at[b], device_id=dev, device_id_type=LOGICAL
        )
        for a, b, dev in plan
    ]


def smooth(src_ref, n, halo, out_ref):
    ylo, yhi, xlo_ref, xhi_ref = halo
    ix, iy = lax.axis_index("gx"), lax.axis_index("gy")
    sub, lane = iota((8, 128), 0), iota((8, 128), 1)
    xlo = jnp.where(ix > 0, xlo_ref[...], 0.0)
    xhi = jnp.where(ix < 3, xhi_ref[...], 0.0)
    zero = jnp.zeros((8, 128), F32)
    for f in range(n):
        for z in range(32):
            j = f * 32 + z
            at = lambda i: src_ref[8 * i : 8 * i + 8, :]
            c = at(j)
            total = (at(j - 1) if z > 0 else zero) + (at(j + 1) if z < 31 else zero)
            low = jnp.where(iy > 0, ylo[j : j + 1, :], 0.0)
            high = jnp.where(iy < 31, yhi[j : j + 1, :], 0.0)
            total += jnp.where(sub == 0, low, pltpu.roll(c, 1, 0))
            total += jnp.where(sub == 7, high, pltpu.roll(c, 7, 0))
            total += jnp.where(lane == 0, pltpu.roll(xlo, (128 - j) % 128, 1), pltpu.roll(c, 1, 1))
            total += jnp.where(lane == 127, pltpu.roll(xhi, (255 - j) % 128, 1), pltpu.roll(c, 127, 1))
            out_ref[8 * j : 8 * j + 8, :] = 0.25 * c + 0.125 * total


def gather(field_ref, cell_ref, seen_ref, f_ref):
    for c in range(4):
        hi, lo = split2(jnp.transpose(field_ref[256 * c : 256 * c + 256, :]))
        f_ref[pl.ds(128 * c, 128), :] = hi
        f_ref[pl.ds(512 + 128 * c, 128), :] = lo

    def step(k, carry):
        cell = row2(cell_ref, k)
        high = hot(iota((256, PB), 0) == (cell >> 7))
        part = dot_nn(f_ref[...], high)
        part = part[:512] + part[512:]
        low = iota((128, PB), 0) == (cell & 127)
        rows = [
            jnp.sum(jnp.where(low, part[128 * c : 128 * c + 128], 0.0), axis=0, keepdims=True)
            for c in range(4)
        ]
        seen_ref[:, pl.ds(pl.multiple_of(k * PB, PB), PB)] = jnp.concatenate(rows, axis=0)
        return carry

    lax.fori_loop(0, NBLK, step, 0)


def deposit_block(rows, cell, acc_ref):
    lo_hot = hot(iota((256, PB), 0) == (cell & 255))
    hi_hot = hot(iota((128, PB), 0) == (cell >> 8))
    left = spread_rows(rows, hi_hot, 128)
    add2(acc_ref, dot_nt(left, lo_hot))


def unfold(acc_ref, n, dep_ref):
    for j in range(2):
        dep_ref[pl.ds(j, n * 128, stride=2), :] = acc_ref[j]


def drag_of(seen_ref, mot_ref, r, lanes):
    return 4.0 / (r * r + 0.25) * (seen_ref[0:3, lanes] - mot_ref[0:3, lanes])


def deposit_four(seen_ref, mot_ref, rad_ref, cell_ref, acc_ref):
    acc_ref[...] = jnp.zeros_like(acc_ref)

    def step(k, carry):
        lanes = pl.ds(pl.multiple_of(k * PB, PB), PB)
        r = row2(rad_ref, k)
        volume = r * r * r
        push = -volume * drag_of(seen_ref, mot_ref, r, lanes)
        deposit_block([volume, push[0:1], push[1:2], push[2:3]], row2(cell_ref, k), acc_ref)
        return carry

    lax.fori_loop(0, NBLK, step, 0)


GROUP = 8


def main_kernel(
    owner_ref, box_ref, pos_ref, mot_ref, rad_ref, tmp_ref, cell_ref, fluid_ref, mask_hbm,
    ret_ref, q_ref, sc_ref, seen_ref, spread_ref,
    rank_ref, acc_ref, sorted_ref, smem_ref, out_ref, got_ref, res_ref, mask_ref,
    field_ref, f_ref, dacc_ref, dep_ref,
    ey0, ey1, ex0, ex1, hy0, hy1, hx0, hx1,
    gy0, gy1, gx0, gx1, ky0, ky1, kx0, kx1,
    table_sem, send_sem, got_sem, back_sem, ret_sem, mask_sem, hs_sem, hr_sem, ks_sem, kr_sem,
):
    me = lax.axis_index("gx") * 32 + lax.axis_index("gy")
    got_ref[...] = jnp.zeros_like(got_ref)
    barrier = pltpu.get_barrier_semaphore()

    def signal(k):
        for i in range(4):
            d = 4 * k + i + 1

            def one():
                pl.semaphore_signal(barrier, inc=1, device_id=lax.rem(me + d, DEV), device_id_type=LOGICAL)

            if i < 3:
                one()
            else:
                pl.when(d < DEV)(one)

    def mask_copy(i):
        part = pl.ds(16 * i, 16)
        return pltpu.make_async_copy(mask_hbm.at[part], mask_ref.at[part], mask_sem.at[i])

    for i in range(8):
        mask_copy(i).start()
    edges(fluid_ref, 4, ey0, ey1, ex0, ex1)
    rank_and_sort(signal, owner_ref, box_ref, pos_ref, mot_ref, rad_ref, tmp_ref, q_ref, sc_ref, rank_ref, acc_ref, sorted_ref, smem_ref, table_sem)
    pl.semaphore_wait(barrier, DEV - 1)
    fluid_halo = halo_copies((ey0, ey1, ex0, ex1), (hy0, hy1, hx0, hx1), hs_sem, hr_sem)
    for copy in fluid_halo:
        copy.start()

    def send(d):
        peer = lax.rem(me + d, DEV)
        return pltpu.make_async_remote_copy(
            out_ref.at[peer, pl.ds(0, 11)], got_ref.at[me, pl.ds(0, 11)],
            send_sem.at[d], got_sem.at[me], device_id=peer, device_id_type=LOGICAL,
        )

    def got(d):
        peer = lax.rem(me + DEV - d, DEV)
        return pltpu.make_async_remote_copy(
            out_ref.at[peer, pl.ds(0, 11)], got_ref.at[peer, pl.ds(0, 11)],
            send_sem.at[d], got_sem.at[peer], device_id=peer, device_id_type=LOGICAL,
        )

    def back(d):
        peer = lax.rem(me + DEV - d, DEV)
        return pltpu.make_async_remote_copy(
            res_ref.at[peer, pl.ds(0, 7)], ret_ref.at[me, pl.ds(0, 7)],
            back_sem.at[d], ret_sem.at[me], device_id=peer, device_id_type=LOGICAL,
        )

    def returned(d):
        peer = lax.rem(me + d, DEV)
        return pltpu.make_async_remote_copy(
            res_ref.at[peer, pl.ds(0, 7)], ret_ref.at[peer, pl.ds(0, 7)],
            back_sem.at[d], ret_sem.at[peer], device_id=peer, device_id_type=LOGICAL,
        )

    def fill(first):
        peers = [lax.rem(me + first + k, DEV) for k in range(GROUP)]
        rows = [window(sorted_ref, smem_ref, p) for p in peers]
        for p, r in zip(peers, rows):
            out_ref[p] = r

    def send_group(first, skip):
        for k in range(skip, GROUP):
            send(first + k).start()

    fill(0)
    got_ref[me] = out_ref[me]
    fill(GROUP)
    send_group(0, 1)

    def fill_and_send(g, carry):
        fill(g * GROUP)
        send_group(g * GROUP - GROUP, 0)
        return carry

    lax.fori_loop(2, DEV // GROUP, fill_and_send, 0)
    send_group(DEV - GROUP, 0)
    for copy in fluid_halo:
        copy.wait()
    smooth(fluid_ref, 4, (hy0, hy1, hx0, hx1), field_ref)
    gather(field_ref, cell_ref, seen_ref, f_ref)
    for i in range(8):
        mask_copy(i).wait()

    def contacts(first):
        peers = [lax.rem(me + DEV - (first + k), DEV) for k in range(GROUP)]
        given = [got_ref[p] for p in peers]
        results = [contact_block(s, mask_ref[p]) for s, p in zip(given, peers)]
        for p, r in zip(peers, results):
            res_ref[p] = r

    def await_group(first, skip):
        for k in range(skip, GROUP):
            got(first + k).wait_recv()

    def send_back(first, skip):
        for k in range(skip, GROUP):
            back(first + k).start()

    await_group(0, 1)
    contacts(0)
    await_group(GROUP, 0)
    contacts(GROUP)
    send_back(0, 1)

    def group(g, carry):
        await_group(g * GROUP, 0)
        contacts(g * GROUP)
        send_back(g * GROUP - GROUP, 0)
        return carry

    lax.fori_loop(2, DEV // GROUP, group, 0)
    for k in range(GROUP):
        back(DEV - GROUP + k).start()
    ret_ref[me] = res_ref[me]

    deposit_four(seen_ref, mot_ref, rad_ref, cell_ref, dacc_ref)
    unfold(dacc_ref, 4, dep_ref)
    edges(dep_ref, 4, gy0, gy1, gx0, gx1)
    dep_halo = halo_copies((gy0, gy1, gx0, gx1), (ky0, ky1, kx0, kx1), ks_sem, kr_sem)
    for copy in dep_halo:
        copy.start()

    def close(d, carry):
        send(d).wait_send()
        back(d).wait_send()
        returned(d).wait_recv()
        return carry

    lax.fori_loop(1, DEV, close, 0)
    for copy in dep_halo:
        copy.wait()
    smooth(dep_ref, 4, (ky0, ky1, kx0, kx1), spread_ref)


def halo_scratch(n):
    return [VMEM((n * 32, 128), F32), VMEM((n * 32, 128), F32), VMEM((8, 128), F32), VMEM((8, 128), F32)]


def vmem_specs(n):
    return [pl.BlockSpec(memory_space=VMEM)] * n


def main(owner, box, pos, mot, rad, tmp, cell, fluid, mask):
    dma = pltpu.SemaphoreType.DMA
    return pl.pallas_call(
        main_kernel,
        out_shape=(
            jax.ShapeDtypeStruct((DEV, 8, 128), F32),
            jax.ShapeDtypeStruct((64, 128), I32),
            jax.ShapeDtypeStruct((8, 128), I32),
            jax.ShapeDtypeStruct((4, PARTS), F32),
            jax.ShapeDtypeStruct((1024, 128), F32),
        ),
        in_specs=vmem_specs(8) + [pl.BlockSpec(memory_space=pl.ANY)],
        out_specs=tuple(vmem_specs(5)),
        scratch_shapes=[
            VMEM((64, 128), F32),
            VMEM((2, 384, 128), F32),
            VMEM((66, 16, 128), F32),
            pltpu.SMEM((8, 128), I32),
            VMEM((DEV, 16, 128), F32),
            VMEM((DEV, 16, 128), F32),
            VMEM((DEV, 8, 128), F32),
            VMEM((DEV, 128, 128), I32),
            VMEM((1024, 128), F32),
            VMEM((1024, 256), BF16),
            VMEM((2, 512, 128), F32),
            VMEM((1032, 128), F32),
            *halo_scratch(4), *halo_scratch(4), *halo_scratch(4), *halo_scratch(4),
            dma, dma((DEV,)), dma((DEV,)), dma((DEV,)), dma((DEV,)), dma((8,)),
            dma((4,)), dma((4,)), dma((4,)), dma((4,)),
        ],
        compiler_params=pltpu.CompilerParams(collective_id=0, has_side_effects=True),
        name="main",
    )(owner, box, pos, mot, rad, tmp, cell, fluid, mask)


def fetch_kernel(
    owner_ref, sc_ref, q_ref, cell_ref, ret_ref, seen_ref, mot_ref, rad_ref, tmp_ref, spread_ref, fluid_ref,
    next_ref, dep_ref, fluid_next_ref, void_ref,
    dense_ref, left_ref, acc_ref,
):
    lane = iota((8, 128), 1)

    def pack(b, open_tile):
        start, after = sc_ref[0, b], sc_ref[0, jnp.minimum(b + 1, DEV - 1)]
        tile, off = jnp.clip(start >> 7, 0, 64), start & 127
        mine = pltpu.roll(ret_ref[owner_ref[b]], off, 1)
        merged = jnp.where(lane < off, open_tile, mine)
        dense_ref[tile] = merged
        return jnp.where((after >> 7) == (start >> 7), merged, mine)

    lax.fori_loop(0, DEV, pack, jnp.zeros((8, 128), F32), unroll=8)
    hi, lo = split2(dense_ref[0:64].reshape(512, 128))
    left_ref[:, 0:128] = hi
    left_ref[:, 128:256] = lo
    acc_ref[...] = jnp.zeros_like(acc_ref)

    def step(k, carry):
        lanes = pl.ds(pl.multiple_of(k * PB, PB), PB)
        q = row2(q_ref, k)
        low = hot(iota((128, PB), 0) == (q & 127))
        part = dot_nn(left_ref[...], jnp.concatenate([low, low], axis=0))
        high = jnp.broadcast_to(q >> 7, (8, PB))
        res = part[0:8]
        for t in range(1, 64):
            res = jnp.where(high == t, part[8 * t : 8 * t + 8], res)
        r = row2(rad_ref, k)
        temp = row2(tmp_ref, k)
        gas = seen_ref[3:4, lanes]
        drag = drag_of(seen_ref, mot_ref, r, lanes)
        vn = mot_ref[0:3, lanes] + (res[0:3] + 0.1 * drag) - jnp.where(iota((3, PB), 0) == 2, 0.03, 0.0)
        tn = temp + (res[3:4] + 0.4 * (gas - temp))
        next_ref[0:3, lanes] = vn
        next_ref[3:6, lanes] = res[4:7]
        next_ref[6:7, lanes] = tn
        deposit_block([r * r * r * (tn - gas)], row2(cell_ref, k), acc_ref)
        return carry

    lax.fori_loop(0, NBLK, step, 0)
    unfold(acc_ref, 1, dep_ref)
    crowding = 1.0 + 4.0 * spread_ref[0:256, :]
    void_ref[...] = 1.0 / crowding
    scale = 0.4 * crowding
    for f in range(3):
        at = slice(256 * f, 256 * f + 256)
        fluid_next_ref[at, :] = fluid_ref[at, :] + spread_ref[256 * f + 256 : 256 * f + 512, :] * scale
    fluid_next_ref[768:1024, :] = scale


def fetch(owner, sc, q, cell, ret, seen, mot, rad, tmp, spread, fluid):
    return pl.pallas_call(
        fetch_kernel,
        out_shape=(
            jax.ShapeDtypeStruct((7, PARTS), F32),
            jax.ShapeDtypeStruct((264, 128), F32),
            jax.ShapeDtypeStruct((1024, 128), F32),
            jax.ShapeDtypeStruct((256, 128), F32),
        ),
        in_specs=[pl.BlockSpec(memory_space=pltpu.SMEM)] * 2 + vmem_specs(9),
        out_specs=tuple(vmem_specs(4)),
        scratch_shapes=[VMEM((66, 8, 128), F32), VMEM((512, 256), BF16), VMEM((2, 128, 128), F32)],
        name="fetch",
    )(owner, sc, q, cell, ret, seen, mot, rad, tmp, spread, fluid)


def end_kernel(dep_ref, heat_ref, ey0, ey1, ex0, ex1, hy0, hy1, hx0, hx1, hs_sem, hr_sem):
    barrier = pltpu.get_barrier_semaphore()
    for dev in neighbours():
        pl.semaphore_signal(barrier, inc=1, device_id=dev, device_id_type=LOGICAL)
    edges(dep_ref, 1, ey0, ey1, ex0, ex1)
    pl.semaphore_wait(barrier, 4)
    halo = halo_copies((ey0, ey1, ex0, ex1), (hy0, hy1, hx0, hx1), hs_sem, hr_sem)
    for copy in halo:
        copy.start()
    for copy in halo:
        copy.wait()
    smooth(dep_ref, 1, (hy0, hy1, hx0, hx1), heat_ref)


def end(dep):
    dma = pltpu.SemaphoreType.DMA
    return pl.pallas_call(
        end_kernel,
        out_shape=jax.ShapeDtypeStruct((256, 128), F32),
        in_specs=vmem_specs(1),
        out_specs=pl.BlockSpec(memory_space=VMEM),
        scratch_shapes=[*halo_scratch(1), *halo_scratch(1), dma((4,)), dma((4,))],
        compiler_params=pltpu.CompilerParams(collective_id=1, has_side_effects=True),
        name="end",
    )(dep)


def shards(fluid, pos, mot, rad, tmp, cell, box, box_owner, mask):
    rad2, tmp2 = rad.reshape(64, 128), tmp.reshape(64, 128)
    cell2, box2 = cell.reshape(64, 128), box.reshape(64, 128)
    fluid2 = fluid.reshape(1024, 128)
    ret, q, sc, seen, spread = main(box_owner.reshape(1, 128), box2, pos, mot, rad2, tmp2, cell2, fluid2, mask)
    nxt, dep, fluid_next, void = fetch(box_owner, sc, q, cell2, ret, seen, mot, rad2, tmp2, spread, fluid2)
    heat = end(dep)
    last = fluid2[768:1024] + heat * fluid_next[768:1024]
    fluid_next = lax.dynamic_update_slice(fluid_next, last, (768, 0))
    return fluid_next.reshape(4, 32, 8, 128), void.reshape(32, 8, 128), nxt


def solution(mesh):
    return jax.shard_map(
        shards,
        mesh=mesh,
        in_specs=(
            P(None, None, "gy", "gx"),
            P(None, GX_GY),
            P(None, GX_GY),
            P(GX_GY),
            P(GX_GY),
            P(GX_GY),
            P(GX_GY, None),
            P(),
            P(GX_GY, None, None),
        ),
        out_specs=(P(None, None, "gy", "gx"), P(None, "gy", "gx"), P(None, GX_GY)),
        check_vma=False,
    )
```

```python
import functools

import jax
import jax.numpy as jnp
from jax import lax
from jax.experimental import pallas as pl
from jax.experimental.pallas import tpu as pltpu
from jax.sharding import PartitionSpec as P

GX_GY = ("gx", "gy")
LOGICAL = pl.DeviceIdType.LOGICAL
F32, BF16, I32 = jnp.float32, jnp.bfloat16, jnp.int32
DEV = 128
PARTS = 8192
RB = 256
PB = 2048
NBLK = PARTS // PB
LOG2E = 1.4426950408889634
VMEM = pltpu.VMEM


def iota(shape, dim):
    return lax.broadcasted_iota(I32, shape, dim)


def hot(mask):
    return jnp.where(mask, 1.0, 0.0).astype(BF16)


def split2(x):
    hi = x.astype(BF16)
    lo = (x - hi.astype(F32)).astype(BF16)
    return hi, lo


def dot_nt(a, b):
    return lax.dot_general(a, b, (((1,), (1,)), ((), ())), preferred_element_type=F32)


def dot_nn(a, b):
    return lax.dot_general(a, b, (((1,), (0,)), ((), ())), preferred_element_type=F32)


def dot_tn(a, b):
    return lax.dot_general(a, b, (((0,), (0,)), ((), ())), preferred_element_type=F32)


def row2(ref, k, size=PB):
    n = size // 128
    return jnp.concatenate([ref[pl.ds(n * k + i, 1), :] for i in range(n)], axis=1)


def add2(ref, x):
    n = x.shape[0] // 2
    x = x[:n] + x[n:]
    ref[0, 0:n] += x[:, :128]
    ref[1, 0:n] += x[:, 128:]


def rank_and_sort(signal, owner_ref, box_ref, pos_ref, mot_ref, rad_ref, tmp_ref, q_ref, sc_ref, rank_ref, acc_ref, sorted_ref, smem_ref, sem):
    tri = hot(iota((RB, RB), 0) < iota((RB, RB), 1))

    def rank_step(k, before):
        signal(k)
        box = row2(box_ref, k, RB)
        match = iota((DEV, RB), 0) == box
        within = dot_nn(hot(match), tri)
        rank = jnp.sum(jnp.where(match, within + before, 0.0), axis=0, keepdims=True)
        rank_ref[pl.ds(2 * k, 1), :] = rank[:, :128]
        rank_ref[pl.ds(2 * k + 1, 1), :] = rank[:, 128:]
        return before + jnp.sum(jnp.where(match, 1.0, 0.0), axis=1, keepdims=True)

    counts = lax.fori_loop(0, PARTS // RB, rank_step, jnp.zeros((DEV, 1), F32), unroll=True)
    down, over = iota((DEV, DEV), 0), iota((DEV, DEV), 1)
    wide = jnp.broadcast_to(counts, (DEV, DEV))
    start_row = jnp.sum(jnp.where(down < over, wide, 0.0), axis=0, keepdims=True)
    start_col = jnp.sum(jnp.where(down == over, start_row, 0.0), axis=1, keepdims=True)
    owner_col = jnp.sum(jnp.where(down == over, owner_ref[0:1, :], 0), axis=1, keepdims=True)
    holds = owner_col == over
    start_at = jnp.sum(jnp.where(holds, start_col, 0.0), axis=0, keepdims=True)
    count_at = jnp.sum(jnp.where(holds, counts, 0.0), axis=0, keepdims=True)
    sub = iota((8, DEV), 0)
    sc_ref[...] = jnp.where(sub == 0, start_row, jnp.where(sub == 1, start_at, count_at)).astype(I32)
    copy = pltpu.make_async_copy(sc_ref, smem_ref, sem)
    copy.start()
    table = jnp.broadcast_to(start_row, (64, DEV))
    q = rank_ref[...] + jnp.take_along_axis(table, box_ref[...], axis=1)
    q_ref[...] = q.astype(I32)
    acc_ref[...] = jnp.zeros_like(acc_ref)

    def sort_step(k, carry):
        q = row2(q_ref, k)
        lo_hot = hot(iota((256, PB), 0) == (q & 255))
        hi_hot = hot(iota((32, PB), 0) == (q >> 8))
        lanes = pl.ds(pl.multiple_of(k * PB, PB), PB)
        rows = [pos_ref[c : c + 1, lanes] for c in range(3)]
        rows += [row2(tmp_ref, k)]
        rows += [mot_ref[c : c + 1, lanes] for c in range(3)]
        rows += [row2(rad_ref, k)]
        rows += [mot_ref[c : c + 1, lanes] for c in range(3, 6)]
        left = spread_rows(rows, hi_hot, 32)
        add2(acc_ref, dot_nt(left, lo_hot))
        return carry

    lax.fori_loop(0, NBLK, sort_step, 0)
    for t in range(64):
        sorted_ref[t, 0:11, :] = acc_ref[t % 2, pl.ds(t // 2, 11, stride=32), :]
    copy.wait()


def spread_rows(rows, hi_hot, n):
    his, los = [], []
    for x in rows:
        hi, lo = split2(jnp.broadcast_to(x, (n, PB)))
        his.append(hi * hi_hot)
        los.append(lo * hi_hot)
    return jnp.concatenate(his + los, axis=0)


def window(sorted_ref, smem_ref, o):
    lane = iota((16, 128), 1)
    start = smem_ref[1, o]
    count = smem_ref[2, o]
    tile, off = jnp.clip(start >> 7, 0, 64), start & 127
    shift = (128 - off) & 127
    low = pltpu.roll(sorted_ref[tile], shift, 1)
    high = pltpu.roll(sorted_ref[tile + 1], shift, 1)
    both = jnp.where(lane < 128 - off, low, high)
    return jnp.where(lane < count, both, 0.0)


def contact_block(s, mask):
    sub = iota((8, 128), 0)
    top = s[0:8]
    r = s[7:8]
    occupied = jnp.where(r > 0.0, 1.0, 0.0)
    scale = jnp.where((sub & 3) == 3, 1.4142135623730951, (2.0 * LOG2E) ** 0.5)
    pos4 = jnp.concatenate([s[0:3], r, s[0:3], r], axis=0)
    y = pos4 * scale
    a = y.astype(BF16).astype(F32)
    b = (y - a).astype(BF16).astype(F32)
    c = y - a - b
    first = sub < 4
    is_r = (sub & 3) == 3
    sq = y * y * 0.5
    m = jnp.sum(jnp.where(first & ~is_r, sq, 0.0), axis=0, keepdims=True)
    g = sq[3:4] + 0.5

    def three(v):
        v1 = v.astype(BF16).astype(F32)
        v2 = (v - v1).astype(BF16).astype(F32)
        return v1, v2, v - v1 - v2

    m1, m2, m3 = three(m)
    g1, g2, g3 = three(g)

    def pick(rows):
        out = jnp.zeros((8, 128), F32)
        for i, v in enumerate(rows):
            out = jnp.where(sub == i, v, out)
        return out

    zero = jnp.zeros((8, 128), F32)
    left = jnp.concatenate(
        [a, b, jnp.where(first, a, c), pick([m1, m2, m3, 1.0, 1.0, 1.0]), pick([g1, g2, g3, 1.0, 1.0, 1.0]), zero], axis=0
    ).astype(BF16)
    h1 = jnp.where(first, a, b)
    h3 = jnp.where(first, c, a)
    h4 = pick([-1.0, -1.0, -1.0, -m1, -m2, -m3])
    h5 = pick([1.0, 1.0, 1.0, g1, g2, g3])
    e_cols = jnp.concatenate(
        [jnp.where(is_r, 0.0, h1), jnp.where(is_r, 0.0, h1), jnp.where(is_r, 0.0, h3), h4, zero, zero], axis=0
    )
    r_cols = jnp.concatenate(
        [jnp.where(is_r, h1, 0.0), jnp.where(is_r, h1, 0.0), jnp.where(is_r, h3, 0.0), zero, h5, zero], axis=0
    )
    right = jnp.concatenate([e_cols, r_cols], axis=1).astype(BF16)
    pair = dot_tn(left, right)
    weight = jnp.where(mask != 0, jnp.exp2(pair[:, :128] / pair[:, 128:]), 0.0)
    wh, wl = split2(weight)
    top_o = jnp.where(sub == 7, occupied, top)
    stacked = jnp.concatenate([top_o, s[8:16]], axis=0)
    sh, sl = split2(stacked)
    lhs = jnp.concatenate(
        [jnp.concatenate([sh, sh], axis=1), jnp.concatenate([sl, jnp.zeros_like(sl)], axis=1)], axis=0
    )
    mixed = dot_nt(lhs, jnp.concatenate([wh, wl], axis=1))
    mixed = mixed[0:16] + mixed[16:32]
    ws = mixed[7:8]
    diff = top * ws - mixed[0:8]
    c1 = jnp.where(sub == 3, -0.03, 0.05)
    c2 = jnp.where(sub == 3, 0.0, 0.02)
    spin = s[8:16] - 0.01 * (s[8:16] * ws + mixed[8:16])
    return jnp.where(first, c1 * diff - c2 * pltpu.roll(diff, 4, 0), pltpu.roll(spin, 4, 0))


def edges(src_ref, n, ylow_ref, yhigh_ref, xlow_ref, xhigh_ref):
    lane = iota((8, 128), 1)
    first = jnp.zeros((8, 128), F32)
    last = jnp.zeros((8, 128), F32)
    for j in range(n * 32):
        v = src_ref[8 * j : 8 * j + 8, :]
        ylow_ref[j : j + 1, :] = v[0:1]
        yhigh_ref[j : j + 1, :] = v[7:8]
        first = jnp.where(lane == j, pltpu.roll(v, j, 1), first)
        last = jnp.where(lane == j, pltpu.roll(v, (j + 1) % 128, 1), last)
    xlow_ref[...] = first
    xhigh_ref[...] = last


def neighbours():
    ix, iy = lax.axis_index("gx"), lax.axis_index("gy")
    up_x = lax.rem(ix + 1, 4) * 32 + iy
    down_x = lax.rem(ix + 3, 4) * 32 + iy
    up_y = ix * 32 + lax.rem(iy + 1, 32)
    down_y = ix * 32 + lax.rem(iy + 31, 32)
    return down_y, up_y, down_x, up_x


def halo_copies(mine, theirs, send_sem, recv_sem):
    down_y, up_y, down_x, up_x = neighbours()
    plan = ((0, 1, down_y), (1, 0, up_y), (2, 3, down_x), (3, 2, up_x))
    return [
        pltpu.make_async_remote_copy(
            mine[a], theirs[b], send_sem.at[a], recv_sem.at[b], device_id=dev, device_id_type=LOGICAL
        )
        for a, b, dev in plan
    ]


def smooth(src_ref, n, halo, out_ref):
    ylo, yhi, xlo_ref, xhi_ref = halo
    ix, iy = lax.axis_index("gx"), lax.axis_index("gy")
    sub, lane = iota((8, 128), 0), iota((8, 128), 1)
    xlo = jnp.where(ix > 0, xlo_ref[...], 0.0)
    xhi = jnp.where(ix < 3, xhi_ref[...], 0.0)
    zero = jnp.zeros((8, 128), F32)
    for f in range(n):
        for z in range(32):
            j = f * 32 + z
            at = lambda i: src_ref[8 * i : 8 * i + 8, :]
            c = at(j)
            total = (at(j - 1) if z > 0 else zero) + (at(j + 1) if z < 31 else zero)
            low = jnp.where(iy > 0, ylo[j : j + 1, :], 0.0)
            high = jnp.where(iy < 31, yhi[j : j + 1, :], 0.0)
            total += jnp.where(sub == 0, low, pltpu.roll(c, 1, 0))
            total += jnp.where(sub == 7, high, pltpu.roll(c, 7, 0))
            total += jnp.where(lane == 0, pltpu.roll(xlo, (128 - j) % 128, 1), pltpu.roll(c, 1, 1))
            total += jnp.where(lane == 127, pltpu.roll(xhi, (255 - j) % 128, 1), pltpu.roll(c, 127, 1))
            out_ref[8 * j : 8 * j + 8, :] = 0.25 * c + 0.125 * total


def gather(field_ref, cell_ref, seen_ref, f_ref):
    for c in range(4):
        hi, lo = split2(jnp.transpose(field_ref[256 * c : 256 * c + 256, :]))
        f_ref[pl.ds(128 * c, 128), :] = hi
        f_ref[pl.ds(512 + 128 * c, 128), :] = lo

    def step(k, carry):
        cell = row2(cell_ref, k)
        high = hot(iota((256, PB), 0) == (cell >> 7))
        part = dot_nn(f_ref[...], high)
        part = part[:512] + part[512:]
        low = iota((128, PB), 0) == (cell & 127)
        rows = [
            jnp.sum(jnp.where(low, part[128 * c : 128 * c + 128], 0.0), axis=0, keepdims=True)
            for c in range(4)
        ]
        seen_ref[:, pl.ds(pl.multiple_of(k * PB, PB), PB)] = jnp.concatenate(rows, axis=0)
        return carry

    lax.fori_loop(0, NBLK, step, 0)


def deposit_block(rows, cell, acc_ref):
    lo_hot = hot(iota((256, PB), 0) == (cell & 255))
    hi_hot = hot(iota((128, PB), 0) == (cell >> 8))
    left = spread_rows(rows, hi_hot, 128)
    add2(acc_ref, dot_nt(left, lo_hot))


def unfold(acc_ref, n, dep_ref):
    for j in range(2):
        dep_ref[pl.ds(j, n * 128, stride=2), :] = acc_ref[j]


def drag_of(seen_ref, mot_ref, r, lanes):
    return 4.0 / (r * r + 0.25) * (seen_ref[0:3, lanes] - mot_ref[0:3, lanes])


def deposit_four(seen_ref, mot_ref, rad_ref, cell_ref, acc_ref):
    acc_ref[...] = jnp.zeros_like(acc_ref)

    def step(k, carry):
        lanes = pl.ds(pl.multiple_of(k * PB, PB), PB)
        r = row2(rad_ref, k)
        volume = r * r * r
        push = -volume * drag_of(seen_ref, mot_ref, r, lanes)
        deposit_block([volume, push[0:1], push[1:2], push[2:3]], row2(cell_ref, k), acc_ref)
        return carry

    lax.fori_loop(0, NBLK, step, 0)


GROUP = 16
FILL = 8


def main_kernel(
    owner_ref, box_ref, pos_ref, mot_ref, rad_ref, tmp_ref, cell_ref, fluid_ref, mask_hbm,
    ret_ref, q_ref, sc_ref, seen_ref, spread_ref,
    rank_ref, acc_ref, sorted_ref, smem_ref, out_ref, got_ref, res_ref, mask_ref,
    field_ref, f_ref, dacc_ref, dep_ref,
    ey0, ey1, ex0, ex1, hy0, hy1, hx0, hx1,
    gy0, gy1, gx0, gx1, ky0, ky1, kx0, kx1,
    table_sem, send_sem, got_sem, back_sem, ret_sem, mask_sem, hs_sem, hr_sem, ks_sem, kr_sem,
):
    me = lax.axis_index("gx") * 32 + lax.axis_index("gy")
    got_ref[...] = jnp.zeros_like(got_ref)
    barrier = pltpu.get_barrier_semaphore()

    def signal(k):
        for i in range(4):
            d = 4 * k + i + 1

            def one():
                pl.semaphore_signal(barrier, inc=1, device_id=lax.rem(me + d, DEV), device_id_type=LOGICAL)

            if i < 3:
                one()
            else:
                pl.when(d < DEV)(one)

    def mask_copy(i):
        part = pl.ds(16 * i, 16)
        return pltpu.make_async_copy(mask_hbm.at[part], mask_ref.at[part], mask_sem.at[i])

    for i in range(8):
        mask_copy(i).start()
    edges(fluid_ref, 4, ey0, ey1, ex0, ex1)
    rank_and_sort(signal, owner_ref, box_ref, pos_ref, mot_ref, rad_ref, tmp_ref, q_ref, sc_ref, rank_ref, acc_ref, sorted_ref, smem_ref, table_sem)
    pl.semaphore_wait(barrier, DEV - 1)
    fluid_halo = halo_copies((ey0, ey1, ex0, ex1), (hy0, hy1, hx0, hx1), hs_sem, hr_sem)
    for copy in fluid_halo:
        copy.start()

    def send(d):
        peer = lax.rem(me + d, DEV)
        return pltpu.make_async_remote_copy(
            out_ref.at[peer, pl.ds(0, 11)], got_ref.at[me, pl.ds(0, 11)],
            send_sem, got_sem.at[me], device_id=peer, device_id_type=LOGICAL,
        )

    def got(d):
        peer = lax.rem(me + DEV - d, DEV)
        return pltpu.make_async_remote_copy(
            out_ref.at[peer, pl.ds(0, 11)], got_ref.at[peer, pl.ds(0, 11)],
            send_sem, got_sem.at[peer], device_id=peer, device_id_type=LOGICAL,
        )

    def back(d):
        peer = lax.rem(me + DEV - d, DEV)
        return pltpu.make_async_remote_copy(
            res_ref.at[peer, pl.ds(0, 7)], ret_ref.at[me, pl.ds(0, 7)],
            back_sem, ret_sem, device_id=peer, device_id_type=LOGICAL,
        )

    def fill(first):
        peers = [lax.rem(me + first + k, DEV) for k in range(FILL)]
        rows = [window(sorted_ref, smem_ref, p) for p in peers]
        for p, r in zip(peers, rows):
            out_ref[p] = r

    def send_group(first, skip):
        for k in range(skip, FILL):
            send(first + k).start()

    fill(0)
    got_ref[me] = out_ref[me]
    fill(FILL)
    send_group(0, 1)

    def fill_and_send(g, carry):
        fill(g * FILL)
        send_group(g * FILL - FILL, 0)
        return carry

    lax.fori_loop(2, DEV // FILL, fill_and_send, 0)
    send_group(DEV - FILL, 0)
    for copy in fluid_halo:
        copy.wait()
    smooth(fluid_ref, 4, (hy0, hy1, hx0, hx1), field_ref)
    gather(field_ref, cell_ref, seen_ref, f_ref)
    for i in range(8):
        mask_copy(i).wait()

    def contacts(first):
        peers = [lax.rem(me + DEV - (first + k), DEV) for k in range(GROUP)]
        given = [got_ref[p] for p in peers]
        results = [contact_block(s, mask_ref[p]) for s, p in zip(given, peers)]
        for p, r in zip(peers, results):
            res_ref[p] = r

    def await_group(first, skip):
        for k in range(skip, GROUP):
            got(first + k).wait_recv()

    def send_back(first, skip):
        for k in range(skip, GROUP):
            back(first + k).start()

    await_group(0, 1)
    contacts(0)
    await_group(GROUP, 0)
    contacts(GROUP)
    send_back(0, 1)

    def group(g, carry):
        await_group(g * GROUP, 0)
        contacts(g * GROUP)
        send_back(g * GROUP - GROUP, 0)
        return carry

    lax.fori_loop(2, DEV // GROUP, group, 0)
    for k in range(GROUP):
        back(DEV - GROUP + k).start()
    ret_ref[me] = res_ref[me]

    deposit_four(seen_ref, mot_ref, rad_ref, cell_ref, dacc_ref)
    unfold(dacc_ref, 4, dep_ref)
    edges(dep_ref, 4, gy0, gy1, gx0, gx1)
    dep_halo = halo_copies((gy0, gy1, gx0, gx1), (ky0, ky1, kx0, kx1), ks_sem, kr_sem)
    for copy in dep_halo:
        copy.start()

    others, beside = pl.ds(0, DEV - 1), lax.rem(me + 1, DEV)
    pltpu.make_async_remote_copy(
        out_ref.at[others, pl.ds(0, 11)], got_ref.at[others, pl.ds(0, 11)],
        send_sem, got_sem.at[0], device_id=beside, device_id_type=LOGICAL,
    ).wait_send()
    pltpu.make_async_remote_copy(
        res_ref.at[others, pl.ds(0, 7)], ret_ref.at[others, pl.ds(0, 7)],
        back_sem, ret_sem, device_id=beside, device_id_type=LOGICAL,
    ).wait()
    for copy in dep_halo:
        copy.wait()
    smooth(dep_ref, 4, (ky0, ky1, kx0, kx1), spread_ref)


def halo_scratch(n):
    return [VMEM((n * 32, 128), F32), VMEM((n * 32, 128), F32), VMEM((8, 128), F32), VMEM((8, 128), F32)]


def vmem_specs(n):
    return [pl.BlockSpec(memory_space=VMEM)] * n


def main(owner, box, pos, mot, rad, tmp, cell, fluid, mask):
    dma = pltpu.SemaphoreType.DMA
    return pl.pallas_call(
        main_kernel,
        out_shape=(
            jax.ShapeDtypeStruct((DEV, 8, 128), F32),
            jax.ShapeDtypeStruct((64, 128), I32),
            jax.ShapeDtypeStruct((8, 128), I32),
            jax.ShapeDtypeStruct((4, PARTS), F32),
            jax.ShapeDtypeStruct((1024, 128), F32),
        ),
        in_specs=vmem_specs(8) + [pl.BlockSpec(memory_space=pl.ANY)],
        out_specs=tuple(vmem_specs(5)),
        scratch_shapes=[
            VMEM((64, 128), F32),
            VMEM((2, 384, 128), F32),
            VMEM((66, 16, 128), F32),
            pltpu.SMEM((8, 128), I32),
            VMEM((DEV, 16, 128), F32),
            VMEM((DEV, 16, 128), F32),
            VMEM((DEV, 8, 128), F32),
            VMEM((DEV, 128, 128), I32),
            VMEM((1024, 128), F32),
            VMEM((1024, 256), BF16),
            VMEM((2, 512, 128), F32),
            VMEM((1032, 128), F32),
            *halo_scratch(4), *halo_scratch(4), *halo_scratch(4), *halo_scratch(4),
            dma, dma, dma((DEV,)), dma, dma, dma((8,)),
            dma((4,)), dma((4,)), dma((4,)), dma((4,)),
        ],
        compiler_params=pltpu.CompilerParams(collective_id=0, has_side_effects=True),
        name="main",
    )(owner, box, pos, mot, rad, tmp, cell, fluid, mask)


def fetch_kernel(
    owner_ref, sc_ref, q_ref, cell_ref, ret_ref, seen_ref, mot_ref, rad_ref, tmp_ref, spread_ref, fluid_ref,
    next_ref, dep_ref, fluid_next_ref, void_ref,
    dense_ref, left_ref, acc_ref,
):
    lane = iota((8, 128), 1)

    def pack(b, open_tile):
        start, after = sc_ref[0, b], sc_ref[0, jnp.minimum(b + 1, DEV - 1)]
        tile, off = jnp.clip(start >> 7, 0, 64), start & 127
        mine = pltpu.roll(ret_ref[owner_ref[b]], off, 1)
        merged = jnp.where(lane < off, open_tile, mine)
        dense_ref[tile] = merged
        return jnp.where((after >> 7) == (start >> 7), merged, mine)

    lax.fori_loop(0, DEV, pack, jnp.zeros((8, 128), F32), unroll=8)
    hi, lo = split2(dense_ref[0:64].reshape(512, 128))
    left_ref[:, 0:128] = hi
    left_ref[:, 128:256] = lo
    acc_ref[...] = jnp.zeros_like(acc_ref)

    def step(k, carry):
        lanes = pl.ds(pl.multiple_of(k * PB, PB), PB)
        q = row2(q_ref, k)
        low = hot(iota((128, PB), 0) == (q & 127))
        part = dot_nn(left_ref[...], jnp.concatenate([low, low], axis=0))
        high = jnp.broadcast_to(q >> 7, (8, PB))
        res = part[0:8]
        for t in range(1, 64):
            res = jnp.where(high == t, part[8 * t : 8 * t + 8], res)
        r = row2(rad_ref, k)
        temp = row2(tmp_ref, k)
        gas = seen_ref[3:4, lanes]
        drag = drag_of(seen_ref, mot_ref, r, lanes)
        vn = mot_ref[0:3, lanes] + (res[0:3] + 0.1 * drag) - jnp.where(iota((3, PB), 0) == 2, 0.03, 0.0)
        tn = temp + (res[3:4] + 0.4 * (gas - temp))
        next_ref[0:3, lanes] = vn
        next_ref[3:6, lanes] = res[4:7]
        next_ref[6:7, lanes] = tn
        deposit_block([r * r * r * (tn - gas)], row2(cell_ref, k), acc_ref)
        return carry

    lax.fori_loop(0, NBLK, step, 0)
    unfold(acc_ref, 1, dep_ref)
    crowding = 1.0 + 4.0 * spread_ref[0:256, :]
    void_ref[...] = 1.0 / crowding
    scale = 0.4 * crowding
    for f in range(3):
        at = slice(256 * f, 256 * f + 256)
        fluid_next_ref[at, :] = fluid_ref[at, :] + spread_ref[256 * f + 256 : 256 * f + 512, :] * scale
    fluid_next_ref[768:1024, :] = scale


def fetch(owner, sc, q, cell, ret, seen, mot, rad, tmp, spread, fluid):
    return pl.pallas_call(
        fetch_kernel,
        out_shape=(
            jax.ShapeDtypeStruct((7, PARTS), F32),
            jax.ShapeDtypeStruct((264, 128), F32),
            jax.ShapeDtypeStruct((1024, 128), F32),
            jax.ShapeDtypeStruct((256, 128), F32),
        ),
        in_specs=[pl.BlockSpec(memory_space=pltpu.SMEM)] * 2 + vmem_specs(9),
        out_specs=tuple(vmem_specs(4)),
        scratch_shapes=[VMEM((66, 8, 128), F32), VMEM((512, 256), BF16), VMEM((2, 128, 128), F32)],
        name="fetch",
    )(owner, sc, q, cell, ret, seen, mot, rad, tmp, spread, fluid)


def end_kernel(dep_ref, heat_ref, ey0, ey1, ex0, ex1, hy0, hy1, hx0, hx1, hs_sem, hr_sem):
    barrier = pltpu.get_barrier_semaphore()
    for dev in neighbours():
        pl.semaphore_signal(barrier, inc=1, device_id=dev, device_id_type=LOGICAL)
    edges(dep_ref, 1, ey0, ey1, ex0, ex1)
    pl.semaphore_wait(barrier, 4)
    halo = halo_copies((ey0, ey1, ex0, ex1), (hy0, hy1, hx0, hx1), hs_sem, hr_sem)
    for copy in halo:
        copy.start()
    for copy in halo:
        copy.wait()
    smooth(dep_ref, 1, (hy0, hy1, hx0, hx1), heat_ref)


def end(dep):
    dma = pltpu.SemaphoreType.DMA
    return pl.pallas_call(
        end_kernel,
        out_shape=jax.ShapeDtypeStruct((256, 128), F32),
        in_specs=vmem_specs(1),
        out_specs=pl.BlockSpec(memory_space=VMEM),
        scratch_shapes=[*halo_scratch(1), *halo_scratch(1), dma((4,)), dma((4,))],
        compiler_params=pltpu.CompilerParams(collective_id=1, has_side_effects=True),
        name="end",
    )(dep)


def shards(fluid, pos, mot, rad, tmp, cell, box, box_owner, mask):
    rad2, tmp2 = rad.reshape(64, 128), tmp.reshape(64, 128)
    cell2, box2 = cell.reshape(64, 128), box.reshape(64, 128)
    fluid2 = fluid.reshape(1024, 128)
    ret, q, sc, seen, spread = main(box_owner.reshape(1, 128), box2, pos, mot, rad2, tmp2, cell2, fluid2, mask)
    nxt, dep, fluid_next, void = fetch(box_owner, sc, q, cell2, ret, seen, mot, rad2, tmp2, spread, fluid2)
    heat = end(dep)
    last = fluid2[768:1024] + heat * fluid_next[768:1024]
    fluid_next = lax.dynamic_update_slice(fluid_next, last, (768, 0))
    return fluid_next.reshape(4, 32, 8, 128), void.reshape(32, 8, 128), nxt


def solution(mesh):
    return jax.shard_map(
        shards,
        mesh=mesh,
        in_specs=(
            P(None, None, "gy", "gx"),
            P(None, GX_GY),
            P(None, GX_GY),
            P(GX_GY),
            P(GX_GY),
            P(GX_GY),
            P(GX_GY, None),
            P(),
            P(GX_GY, None, None),
        ),
        out_specs=(P(None, None, "gy", "gx"), P(None, "gy", "gx"), P(None, GX_GY)),
        check_vma=False,
    )
```

```python
import functools

import jax
import jax.numpy as jnp
from jax import lax
from jax.experimental import pallas as pl
from jax.experimental.pallas import tpu as pltpu
from jax.sharding import PartitionSpec as P

GX_GY = ("gx", "gy")
LOGICAL = pl.DeviceIdType.LOGICAL
F32, BF16, I32 = jnp.float32, jnp.bfloat16, jnp.int32
DEV = 128
PARTS = 8192
RB = 256
PB = 4096
NBLK = PARTS // PB
LOG2E = 1.4426950408889634
VMEM = pltpu.VMEM


def iota(shape, dim):
    return lax.broadcasted_iota(I32, shape, dim)


def hot(mask):
    return jnp.where(mask, 1.0, 0.0).astype(BF16)


def split2(x):
    hi = x.astype(BF16)
    lo = (x - hi.astype(F32)).astype(BF16)
    return hi, lo


def dot_nt(a, b):
    return lax.dot_general(a, b, (((1,), (1,)), ((), ())), preferred_element_type=F32)


def dot_nn(a, b):
    return lax.dot_general(a, b, (((1,), (0,)), ((), ())), preferred_element_type=F32)


def dot_tn(a, b):
    return lax.dot_general(a, b, (((0,), (0,)), ((), ())), preferred_element_type=F32)


def row2(ref, k, size=PB):
    n = size // 128
    return jnp.concatenate([ref[pl.ds(n * k + i, 1), :] for i in range(n)], axis=1)


def add2(ref, x):
    n = x.shape[0] // 2
    x = x[:n] + x[n:]
    ref[0, 0:n] += x[:, :128]
    ref[1, 0:n] += x[:, 128:]


def rank_and_sort(signal, owner_ref, box_ref, pos_ref, mot_ref, rad_ref, tmp_ref, q_ref, sc_ref, rank_ref, acc_ref, sorted_ref, smem_ref, sem):
    tri = hot(iota((RB, RB), 0) < iota((RB, RB), 1))

    def rank_step(k, before):
        signal(k)
        box = row2(box_ref, k, RB)
        match = iota((DEV, RB), 0) == box
        within = dot_nn(hot(match), tri)
        rank = jnp.sum(jnp.where(match, within + before, 0.0), axis=0, keepdims=True)
        rank_ref[pl.ds(2 * k, 1), :] = rank[:, :128]
        rank_ref[pl.ds(2 * k + 1, 1), :] = rank[:, 128:]
        return before + jnp.sum(jnp.where(match, 1.0, 0.0), axis=1, keepdims=True)

    counts = lax.fori_loop(0, PARTS // RB, rank_step, jnp.zeros((DEV, 1), F32), unroll=True)
    down, over = iota((DEV, DEV), 0), iota((DEV, DEV), 1)
    wide = jnp.broadcast_to(counts, (DEV, DEV))
    start_row = jnp.sum(jnp.where(down < over, wide, 0.0), axis=0, keepdims=True)
    start_col = jnp.sum(jnp.where(down == over, start_row, 0.0), axis=1, keepdims=True)
    owner_col = jnp.sum(jnp.where(down == over, owner_ref[0:1, :], 0), axis=1, keepdims=True)
    holds = owner_col == over
    start_at = jnp.sum(jnp.where(holds, start_col, 0.0), axis=0, keepdims=True)
    count_at = jnp.sum(jnp.where(holds, counts, 0.0), axis=0, keepdims=True)
    sub = iota((8, DEV), 0)
    sc_ref[...] = jnp.where(sub == 0, start_row, jnp.where(sub == 1, start_at, count_at)).astype(I32)
    copy = pltpu.make_async_copy(sc_ref, smem_ref, sem)
    copy.start()
    table = jnp.broadcast_to(start_row, (64, DEV))
    q = rank_ref[...] + jnp.take_along_axis(table, box_ref[...], axis=1)
    q_ref[...] = q.astype(I32)
    acc_ref[...] = jnp.zeros_like(acc_ref)

    def sort_step(k, carry):
        q = row2(q_ref, k)
        lo_hot = hot(iota((256, PB), 0) == (q & 255))
        hi_hot = hot(iota((32, PB), 0) == (q >> 8))
        lanes = pl.ds(pl.multiple_of(k * PB, PB), PB)
        rows = [pos_ref[c : c + 1, lanes] for c in range(3)]
        rows += [row2(tmp_ref, k)]
        rows += [mot_ref[c : c + 1, lanes] for c in range(3)]
        rows += [row2(rad_ref, k)]
        rows += [mot_ref[c : c + 1, lanes] for c in range(3, 6)]
        left = spread_rows(rows, hi_hot, 32)
        add2(acc_ref, dot_nt(left, lo_hot))
        return carry

    lax.fori_loop(0, NBLK, sort_step, 0)
    for t in range(64):
        sorted_ref[t, 0:11, :] = acc_ref[t % 2, pl.ds(t // 2, 11, stride=32), :]
    copy.wait()


def spread_rows(rows, hi_hot, n):
    his, los = [], []
    for x in rows:
        hi, lo = split2(jnp.broadcast_to(x, (n, PB)))
        his.append(hi * hi_hot)
        los.append(lo * hi_hot)
    return jnp.concatenate(his + los, axis=0)


def window(sorted_ref, smem_ref, o):
    lane = iota((16, 128), 1)
    start = smem_ref[1, o]
    count = smem_ref[2, o]
    tile, off = jnp.clip(start >> 7, 0, 64), start & 127
    shift = (128 - off) & 127
    low = pltpu.roll(sorted_ref[tile], shift, 1)
    high = pltpu.roll(sorted_ref[tile + 1], shift, 1)
    both = jnp.where(lane < 128 - off, low, high)
    return jnp.where(lane < count, both, 0.0)


def contact_block(s, mask):
    sub = iota((8, 128), 0)
    top = s[0:8]
    r = s[7:8]
    occupied = jnp.where(r > 0.0, 1.0, 0.0)
    scale = jnp.where((sub & 3) == 3, 1.4142135623730951, (2.0 * LOG2E) ** 0.5)
    pos4 = jnp.concatenate([s[0:3], r, s[0:3], r], axis=0)
    y = pos4 * scale
    a = y.astype(BF16).astype(F32)
    b = (y - a).astype(BF16).astype(F32)
    c = y - a - b
    first = sub < 4
    is_r = (sub & 3) == 3
    sq = y * y * 0.5
    m = jnp.sum(jnp.where(first & ~is_r, sq, 0.0), axis=0, keepdims=True)
    g = sq[3:4] + 0.5

    def three(v):
        v1 = v.astype(BF16).astype(F32)
        v2 = (v - v1).astype(BF16).astype(F32)
        return v1, v2, v - v1 - v2

    m1, m2, m3 = three(m)
    g1, g2, g3 = three(g)

    def pick(rows):
        out = jnp.zeros((8, 128), F32)
        for i, v in enumerate(rows):
            out = jnp.where(sub == i, v, out)
        return out

    zero = jnp.zeros((8, 128), F32)
    left = jnp.concatenate(
        [a, b, jnp.where(first, a, c), pick([m1, m2, m3, 1.0, 1.0, 1.0]), pick([g1, g2, g3, 1.0, 1.0, 1.0]), zero], axis=0
    ).astype(BF16)
    h1 = jnp.where(first, a, b)
    h3 = jnp.where(first, c, a)
    h4 = pick([-1.0, -1.0, -1.0, -m1, -m2, -m3])
    h5 = pick([1.0, 1.0, 1.0, g1, g2, g3])
    e_cols = jnp.concatenate(
        [jnp.where(is_r, 0.0, h1), jnp.where(is_r, 0.0, h1), jnp.where(is_r, 0.0, h3), h4, zero, zero], axis=0
    )
    r_cols = jnp.concatenate(
        [jnp.where(is_r, h1, 0.0), jnp.where(is_r, h1, 0.0), jnp.where(is_r, h3, 0.0), zero, h5, zero], axis=0
    )
    right = jnp.concatenate([e_cols, r_cols], axis=1).astype(BF16)
    pair = dot_tn(left, right)
    weight = jnp.where(mask != 0, jnp.exp2(pair[:, :128] / pair[:, 128:]), 0.0)
    wh, wl = split2(weight)
    top_o = jnp.where(sub == 7, occupied, top)
    stacked = jnp.concatenate([top_o, s[8:16]], axis=0)
    sh, sl = split2(stacked)
    lhs = jnp.concatenate(
        [jnp.concatenate([sh, sh], axis=1), jnp.concatenate([sl, jnp.zeros_like(sl)], axis=1)], axis=0
    )
    mixed = dot_nt(lhs, jnp.concatenate([wh, wl], axis=1))
    mixed = mixed[0:16] + mixed[16:32]
    ws = mixed[7:8]
    diff = top * ws - mixed[0:8]
    c1 = jnp.where(sub == 3, -0.03, 0.05)
    c2 = jnp.where(sub == 3, 0.0, 0.02)
    spin = s[8:16] - 0.01 * (s[8:16] * ws + mixed[8:16])
    return jnp.where(first, c1 * diff - c2 * pltpu.roll(diff, 4, 0), pltpu.roll(spin, 4, 0))


def edges(src_ref, n, ylow_ref, yhigh_ref, xlow_ref, xhigh_ref):
    lane = iota((8, 128), 1)
    first = jnp.zeros((8, 128), F32)
    last = jnp.zeros((8, 128), F32)
    for j in range(n * 32):
        v = src_ref[8 * j : 8 * j + 8, :]
        ylow_ref[j : j + 1, :] = v[0:1]
        yhigh_ref[j : j + 1, :] = v[7:8]
        first = jnp.where(lane == j, pltpu.roll(v, j, 1), first)
        last = jnp.where(lane == j, pltpu.roll(v, (j + 1) % 128, 1), last)
    xlow_ref[...] = first
    xhigh_ref[...] = last


def neighbours():
    ix, iy = lax.axis_index("gx"), lax.axis_index("gy")
    up_x = lax.rem(ix + 1, 4) * 32 + iy
    down_x = lax.rem(ix + 3, 4) * 32 + iy
    up_y = ix * 32 + lax.rem(iy + 1, 32)
    down_y = ix * 32 + lax.rem(iy + 31, 32)
    return down_y, up_y, down_x, up_x


def halo_copies(mine, theirs, send_sem, recv_sem):
    down_y, up_y, down_x, up_x = neighbours()
    plan = ((0, 1, down_y), (1, 0, up_y), (2, 3, down_x), (3, 2, up_x))
    return [
        pltpu.make_async_remote_copy(
            mine[a], theirs[b], send_sem.at[a], recv_sem.at[b], device_id=dev, device_id_type=LOGICAL
        )
        for a, b, dev in plan
    ]


def smooth(src_ref, n, halo, out_ref):
    ylo, yhi, xlo_ref, xhi_ref = halo
    ix, iy = lax.axis_index("gx"), lax.axis_index("gy")
    sub, lane = iota((8, 128), 0), iota((8, 128), 1)
    xlo = jnp.where(ix > 0, xlo_ref[...], 0.0)
    xhi = jnp.where(ix < 3, xhi_ref[...], 0.0)
    zero = jnp.zeros((8, 128), F32)
    for f in range(n):
        for z in range(32):
            j = f * 32 + z
            at = lambda i: src_ref[8 * i : 8 * i + 8, :]
            c = at(j)
            total = (at(j - 1) if z > 0 else zero) + (at(j + 1) if z < 31 else zero)
            low = jnp.where(iy > 0, ylo[j : j + 1, :], 0.0)
            high = jnp.where(iy < 31, yhi[j : j + 1, :], 0.0)
            total += jnp.where(sub == 0, low, pltpu.roll(c, 1, 0))
            total += jnp.where(sub == 7, high, pltpu.roll(c, 7, 0))
            total += jnp.where(lane == 0, pltpu.roll(xlo, (128 - j) % 128, 1), pltpu.roll(c, 1, 1))
            total += jnp.where(lane == 127, pltpu.roll(xhi, (255 - j) % 128, 1), pltpu.roll(c, 127, 1))
            out_ref[8 * j : 8 * j + 8, :] = 0.25 * c + 0.125 * total


def gather(field_ref, cell_ref, seen_ref, f_ref):
    for c in range(4):
        hi, lo = split2(jnp.transpose(field_ref[256 * c : 256 * c + 256, :]))
        f_ref[pl.ds(128 * c, 128), :] = hi
        f_ref[pl.ds(512 + 128 * c, 128), :] = lo

    def step(k, carry):
        cell = row2(cell_ref, k)
        high = hot(iota((256, PB), 0) == (cell >> 7))
        part = dot_nn(f_ref[...], high)
        part = part[:512] + part[512:]
        low = iota((128, PB), 0) == (cell & 127)
        rows = [
            jnp.sum(jnp.where(low, part[128 * c : 128 * c + 128], 0.0), axis=0, keepdims=True)
            for c in range(4)
        ]
        seen_ref[:, pl.ds(pl.multiple_of(k * PB, PB), PB)] = jnp.concatenate(rows, axis=0)
        return carry

    lax.fori_loop(0, NBLK, step, 0)


def deposit_block(rows, cell, acc_ref):
    lo_hot = hot(iota((256, PB), 0) == (cell & 255))
    hi_hot = hot(iota((128, PB), 0) == (cell >> 8))
    left = spread_rows(rows, hi_hot, 128)
    add2(acc_ref, dot_nt(left, lo_hot))


def unfold(acc_ref, n, dep_ref):
    for j in range(2):
        dep_ref[pl.ds(j, n * 128, stride=2), :] = acc_ref[j]


def drag_of(seen_ref, mot_ref, r, lanes):
    return 4.0 / (r * r + 0.25) * (seen_ref[0:3, lanes] - mot_ref[0:3, lanes])


def deposit_four(seen_ref, mot_ref, rad_ref, cell_ref, acc_ref):
    acc_ref[...] = jnp.zeros_like(acc_ref)

    def step(k, carry):
        lanes = pl.ds(pl.multiple_of(k * PB, PB), PB)
        r = row2(rad_ref, k)
        volume = r * r * r
        push = -volume * drag_of(seen_ref, mot_ref, r, lanes)
        deposit_block([volume, push[0:1], push[1:2], push[2:3]], row2(cell_ref, k), acc_ref)
        return carry

    lax.fori_loop(0, NBLK, step, 0)


GROUP = 16
FILL = 8


def main_kernel(
    owner_ref, box_ref, pos_ref, mot_ref, rad_ref, tmp_ref, cell_ref, fluid_ref, mask_hbm,
    ret_ref, q_ref, sc_ref, seen_ref, spread_ref,
    rank_ref, acc_ref, sorted_ref, smem_ref, out_ref, got_ref, res_ref, mask_ref,
    field_ref, f_ref, dacc_ref, dep_ref,
    ey0, ey1, ex0, ex1, hy0, hy1, hx0, hx1,
    gy0, gy1, gx0, gx1, ky0, ky1, kx0, kx1,
    table_sem, send_sem, got_sem, back_sem, ret_sem, mask_sem, hs_sem, hr_sem, ks_sem, kr_sem,
):
    me = lax.axis_index("gx") * 32 + lax.axis_index("gy")
    got_ref[...] = jnp.zeros_like(got_ref)
    barrier = pltpu.get_barrier_semaphore()

    def signal(k):
        for i in range(4):
            d = 4 * k + i + 1

            def one():
                pl.semaphore_signal(barrier, inc=1, device_id=lax.rem(me + d, DEV), device_id_type=LOGICAL)

            if i < 3:
                one()
            else:
                pl.when(d < DEV)(one)

    def mask_copy(i):
        part = pl.ds(16 * i, 16)
        return pltpu.make_async_copy(mask_hbm.at[part], mask_ref.at[part], mask_sem.at[i])

    for i in range(8):
        mask_copy(i).start()
    edges(fluid_ref, 4, ey0, ey1, ex0, ex1)
    rank_and_sort(signal, owner_ref, box_ref, pos_ref, mot_ref, rad_ref, tmp_ref, q_ref, sc_ref, rank_ref, acc_ref, sorted_ref, smem_ref, table_sem)
    pl.semaphore_wait(barrier, DEV - 1)
    fluid_halo = halo_copies((ey0, ey1, ex0, ex1), (hy0, hy1, hx0, hx1), hs_sem, hr_sem)
    for copy in fluid_halo:
        copy.start()

    def send(d):
        peer = lax.rem(me + d, DEV)
        return pltpu.make_async_remote_copy(
            out_ref.at[peer, pl.ds(0, 11)], got_ref.at[me, pl.ds(0, 11)],
            send_sem, got_sem.at[me], device_id=peer, device_id_type=LOGICAL,
        )

    def got(d):
        peer = lax.rem(me + DEV - d, DEV)
        return pltpu.make_async_remote_copy(
            out_ref.at[peer, pl.ds(0, 11)], got_ref.at[peer, pl.ds(0, 11)],
            send_sem, got_sem.at[peer], device_id=peer, device_id_type=LOGICAL,
        )

    def back(d):
        peer = lax.rem(me + DEV - d, DEV)
        return pltpu.make_async_remote_copy(
            res_ref.at[peer, pl.ds(0, 7)], ret_ref.at[me, pl.ds(0, 7)],
            back_sem, ret_sem, device_id=peer, device_id_type=LOGICAL,
        )

    def fill(first):
        peers = [lax.rem(me + first + k, DEV) for k in range(FILL)]
        rows = [window(sorted_ref, smem_ref, p) for p in peers]
        for p, r in zip(peers, rows):
            out_ref[p] = r

    def send_group(first, skip):
        for k in range(skip, FILL):
            send(first + k).start()

    fill(0)
    got_ref[me] = out_ref[me]
    fill(FILL)
    send_group(0, 1)

    def fill_and_send(g, carry):
        fill(g * FILL)
        send_group(g * FILL - FILL, 0)
        return carry

    lax.fori_loop(2, DEV // FILL, fill_and_send, 0)
    send_group(DEV - FILL, 0)
    for copy in fluid_halo:
        copy.wait()
    smooth(fluid_ref, 4, (hy0, hy1, hx0, hx1), field_ref)
    gather(field_ref, cell_ref, seen_ref, f_ref)
    for i in range(8):
        mask_copy(i).wait()

    def contacts(first):
        peers = [lax.rem(me + DEV - (first + k), DEV) for k in range(GROUP)]
        given = [got_ref[p] for p in peers]
        results = [contact_block(s, mask_ref[p]) for s, p in zip(given, peers)]
        for p, r in zip(peers, results):
            res_ref[p] = r

    def await_group(first, skip):
        for k in range(skip, GROUP):
            got(first + k).wait_recv()

    def send_back(first, skip):
        for k in range(skip, GROUP):
            back(first + k).start()

    await_group(0, 1)
    contacts(0)
    await_group(GROUP, 0)
    contacts(GROUP)
    send_back(0, 1)

    def group(g, carry):
        await_group(g * GROUP, 0)
        contacts(g * GROUP)
        send_back(g * GROUP - GROUP, 0)
        return carry

    lax.fori_loop(2, DEV // GROUP, group, 0)
    for k in range(GROUP):
        back(DEV - GROUP + k).start()
    ret_ref[me] = res_ref[me]

    deposit_four(seen_ref, mot_ref, rad_ref, cell_ref, dacc_ref)
    unfold(dacc_ref, 4, dep_ref)
    edges(dep_ref, 4, gy0, gy1, gx0, gx1)
    dep_halo = halo_copies((gy0, gy1, gx0, gx1), (ky0, ky1, kx0, kx1), ks_sem, kr_sem)
    for copy in dep_halo:
        copy.start()

    others, beside = pl.ds(0, DEV - 1), lax.rem(me + 1, DEV)
    pltpu.make_async_remote_copy(
        out_ref.at[others, pl.ds(0, 11)], got_ref.at[others, pl.ds(0, 11)],
        send_sem, got_sem.at[0], device_id=beside, device_id_type=LOGICAL,
    ).wait_send()
    pltpu.make_async_remote_copy(
        res_ref.at[others, pl.ds(0, 7)], ret_ref.at[others, pl.ds(0, 7)],
        back_sem, ret_sem, device_id=beside, device_id_type=LOGICAL,
    ).wait()
    for copy in dep_halo:
        copy.wait()
    smooth(dep_ref, 4, (ky0, ky1, kx0, kx1), spread_ref)


def halo_scratch(n):
    return [VMEM((n * 32, 128), F32), VMEM((n * 32, 128), F32), VMEM((8, 128), F32), VMEM((8, 128), F32)]


def vmem_specs(n):
    return [pl.BlockSpec(memory_space=VMEM)] * n


def main(owner, box, pos, mot, rad, tmp, cell, fluid, mask):
    dma = pltpu.SemaphoreType.DMA
    return pl.pallas_call(
        main_kernel,
        out_shape=(
            jax.ShapeDtypeStruct((DEV, 8, 128), F32),
            jax.ShapeDtypeStruct((64, 128), I32),
            jax.ShapeDtypeStruct((8, 128), I32),
            jax.ShapeDtypeStruct((4, PARTS), F32),
            jax.ShapeDtypeStruct((1024, 128), F32),
        ),
        in_specs=vmem_specs(8) + [pl.BlockSpec(memory_space=pl.ANY)],
        out_specs=tuple(vmem_specs(5)),
        scratch_shapes=[
            VMEM((64, 128), F32),
            VMEM((2, 384, 128), F32),
            VMEM((66, 16, 128), F32),
            pltpu.SMEM((8, 128), I32),
            VMEM((DEV, 16, 128), F32),
            VMEM((DEV, 16, 128), F32),
            VMEM((DEV, 8, 128), F32),
            VMEM((DEV, 128, 128), I32),
            VMEM((1024, 128), F32),
            VMEM((1024, 256), BF16),
            VMEM((2, 512, 128), F32),
            VMEM((1032, 128), F32),
            *halo_scratch(4), *halo_scratch(4), *halo_scratch(4), *halo_scratch(4),
            dma, dma, dma((DEV,)), dma, dma, dma((8,)),
            dma((4,)), dma((4,)), dma((4,)), dma((4,)),
        ],
        compiler_params=pltpu.CompilerParams(collective_id=0, has_side_effects=True),
        name="main",
    )(owner, box, pos, mot, rad, tmp, cell, fluid, mask)


def fetch_kernel(
    owner_ref, sc_ref, q_ref, cell_ref, ret_ref, seen_ref, mot_ref, rad_ref, tmp_ref, spread_ref, fluid_ref,
    next_ref, dep_ref, fluid_next_ref, void_ref,
    dense_ref, left_ref, acc_ref,
):
    lane = iota((8, 128), 1)

    def pack(b, open_tile):
        start, after = sc_ref[0, b], sc_ref[0, jnp.minimum(b + 1, DEV - 1)]
        tile, off = jnp.clip(start >> 7, 0, 64), start & 127
        mine = pltpu.roll(ret_ref[owner_ref[b]], off, 1)
        merged = jnp.where(lane < off, open_tile, mine)
        dense_ref[tile] = merged
        return jnp.where((after >> 7) == (start >> 7), merged, mine)

    lax.fori_loop(0, DEV, pack, jnp.zeros((8, 128), F32), unroll=8)
    hi, lo = split2(dense_ref[0:64].reshape(512, 128))
    left_ref[:, 0:128] = hi
    left_ref[:, 128:256] = lo
    acc_ref[...] = jnp.zeros_like(acc_ref)

    def step(k, carry):
        lanes = pl.ds(pl.multiple_of(k * PB, PB), PB)
        q = row2(q_ref, k)
        low = hot(iota((128, PB), 0) == (q & 127))
        part = dot_nn(left_ref[...], jnp.concatenate([low, low], axis=0))
        high = jnp.broadcast_to(q >> 7, (8, PB))
        res = part[0:8]
        for t in range(1, 64):
            res = jnp.where(high == t, part[8 * t : 8 * t + 8], res)
        r = row2(rad_ref, k)
        temp = row2(tmp_ref, k)
        gas = seen_ref[3:4, lanes]
        drag = drag_of(seen_ref, mot_ref, r, lanes)
        vn = mot_ref[0:3, lanes] + (res[0:3] + 0.1 * drag) - jnp.where(iota((3, PB), 0) == 2, 0.03, 0.0)
        tn = temp + (res[3:4] + 0.4 * (gas - temp))
        next_ref[0:3, lanes] = vn
        next_ref[3:6, lanes] = res[4:7]
        next_ref[6:7, lanes] = tn
        deposit_block([r * r * r * (tn - gas)], row2(cell_ref, k), acc_ref)
        return carry

    lax.fori_loop(0, NBLK, step, 0)
    unfold(acc_ref, 1, dep_ref)
    crowding = 1.0 + 4.0 * spread_ref[0:256, :]
    void_ref[...] = 1.0 / crowding
    scale = 0.4 * crowding
    for f in range(3):
        at = slice(256 * f, 256 * f + 256)
        fluid_next_ref[at, :] = fluid_ref[at, :] + spread_ref[256 * f + 256 : 256 * f + 512, :] * scale
    fluid_next_ref[768:1024, :] = scale


def fetch(owner, sc, q, cell, ret, seen, mot, rad, tmp, spread, fluid):
    return pl.pallas_call(
        fetch_kernel,
        out_shape=(
            jax.ShapeDtypeStruct((7, PARTS), F32),
            jax.ShapeDtypeStruct((264, 128), F32),
            jax.ShapeDtypeStruct((1024, 128), F32),
            jax.ShapeDtypeStruct((256, 128), F32),
        ),
        in_specs=[pl.BlockSpec(memory_space=pltpu.SMEM)] * 2 + vmem_specs(9),
        out_specs=tuple(vmem_specs(4)),
        scratch_shapes=[VMEM((66, 8, 128), F32), VMEM((512, 256), BF16), VMEM((2, 128, 128), F32)],
        name="fetch",
    )(owner, sc, q, cell, ret, seen, mot, rad, tmp, spread, fluid)


def end_kernel(dep_ref, heat_ref, ey0, ey1, ex0, ex1, hy0, hy1, hx0, hx1, hs_sem, hr_sem):
    barrier = pltpu.get_barrier_semaphore()
    for dev in neighbours():
        pl.semaphore_signal(barrier, inc=1, device_id=dev, device_id_type=LOGICAL)
    edges(dep_ref, 1, ey0, ey1, ex0, ex1)
    pl.semaphore_wait(barrier, 4)
    halo = halo_copies((ey0, ey1, ex0, ex1), (hy0, hy1, hx0, hx1), hs_sem, hr_sem)
    for copy in halo:
        copy.start()
    for copy in halo:
        copy.wait()
    smooth(dep_ref, 1, (hy0, hy1, hx0, hx1), heat_ref)


def end(dep):
    dma = pltpu.SemaphoreType.DMA
    return pl.pallas_call(
        end_kernel,
        out_shape=jax.ShapeDtypeStruct((256, 128), F32),
        in_specs=vmem_specs(1),
        out_specs=pl.BlockSpec(memory_space=VMEM),
        scratch_shapes=[*halo_scratch(1), *halo_scratch(1), dma((4,)), dma((4,))],
        compiler_params=pltpu.CompilerParams(collective_id=1, has_side_effects=True),
        name="end",
    )(dep)


def shards(fluid, pos, mot, rad, tmp, cell, box, box_owner, mask):
    rad2, tmp2 = rad.reshape(64, 128), tmp.reshape(64, 128)
    cell2, box2 = cell.reshape(64, 128), box.reshape(64, 128)
    fluid2 = fluid.reshape(1024, 128)
    ret, q, sc, seen, spread = main(box_owner.reshape(1, 128), box2, pos, mot, rad2, tmp2, cell2, fluid2, mask)
    nxt, dep, fluid_next, void = fetch(box_owner, sc, q, cell2, ret, seen, mot, rad2, tmp2, spread, fluid2)
    heat = end(dep)
    last = fluid2[768:1024] + heat * fluid_next[768:1024]
    fluid_next = lax.dynamic_update_slice(fluid_next, last, (768, 0))
    return fluid_next.reshape(4, 32, 8, 128), void.reshape(32, 8, 128), nxt


def solution(mesh):
    return jax.shard_map(
        shards,
        mesh=mesh,
        in_specs=(
            P(None, None, "gy", "gx"),
            P(None, GX_GY),
            P(None, GX_GY),
            P(GX_GY),
            P(GX_GY),
            P(GX_GY),
            P(GX_GY, None),
            P(),
            P(GX_GY, None, None),
        ),
        out_specs=(P(None, None, "gy", "gx"), P(None, "gy", "gx"), P(None, GX_GY)),
        check_vma=False,
    )
```
